32 devices in a mesh: ctx: 8 (over z, y), fsdp: 4 (over x, core).
Axes of the slice: x: 2, y: 2, z: 4, core: 2. Of those that a mesh axis runs over, the one named last changes fastest.
Arguments:
- tokens: bfloat16 [2048, 4096], P('ctx', 'fsdp'), may hold values from -150 to 150
- norm_gain: float32 [4096], replicated, may hold values from 0.1 to 1.9
- in_weight: bfloat16 [4096, 3, 4096], P('ctx', None, 'fsdp'), may hold values from -0.09375 to 0.09375
- short_filter: float32 [3, 3, 4096], P(None, None, 'fsdp'), may hold values from -3.5 to 3.5
- long_filter: bfloat16 [256, 128], P('fsdp'), may hold values from -0.5 to 0.5
- skip_gain: float32 [4096], P('fsdp'), may hold values from -4 to 4
- out_weight: bfloat16 [4096, 4096], P('fsdp', 'ctx'), may hold values from -0.09375 to 0.09375
Outputs:
- mixed: bfloat16 [2048, 4096], P('ctx', 'fsdp')
The draws below stay inside these ranges and needn't reach their ends.
All inputs are finite; a program needn't handle non-finite values.
Results may differ from the reference program's by a relative error of at most 0.0091.
Values may be sent and summed in bfloat16 or wider, within the bound.
A program may use at most 128 MiB of HBM per device.

```python
import math
import jax
import jax.numpy as jnp
from jax import lax

D = 4096
GROUP = 16
GROUPS_WIN = 256
FLEN = 128
CH = 4096
SEQ = 2048


def draw_tokens(key, part):
    first = jax.random.fold_in(key, 11)
    second = jax.random.fold_in(key, 12)
    third = jax.random.fold_in(key, 13)
    base = jnp.clip(jax.random.normal(first, (SEQ, D), jnp.float32), -5.0, 5.0)
    row_scale = jnp.exp(jax.random.uniform(second, (SEQ, 1), jnp.float32, 0.0, math.log(10.0)))
    col_scale = jnp.exp(jax.random.uniform(third, (1, D), jnp.float32, math.log(0.3), math.log(3.0)))
    return (base * row_scale * col_scale).astype(jnp.bfloat16)


def levels(own_key, dims, shards, least, high):
    loudness, own = 1.0, jax.random.fold_in(own_key, 6)
    for dim, parts in shards:
        draws = jnp.exp(jax.random.uniform(jax.random.fold_in(own, dim), (parts,), jnp.float32, least / len(shards), high / len(shards)))
        loudness = loudness * jnp.repeat(draws, dims[dim] // parts).reshape([-1 if axis == dim else 1 for axis in range(len(dims))])
    return loudness


def gaussian(stream_key, dims, width, reach, cuts=(), held_as=jnp.bfloat16):
    values = width * jax.random.normal(stream_key, dims, jnp.float32)
    if cuts:
        values = values * levels(stream_key, dims, cuts, -0.22, 0.18)
    return jnp.clip(values, -reach, reach).astype(held_as)


def setup_inputs(seed: int = 0) -> dict:
    key_of = jax.random.split(jax.random.key(seed), 8)
    tokens = draw_tokens(jax.random.fold_in(key_of[7], 71), 0)
    norm_gain = jnp.clip(1.0 + 0.18 * jax.random.normal(key_of[1], (D,), jnp.float32), 0.1, 1.9)
    in_weight = gaussian(key_of[2], (D, 3, CH), D ** -0.5, 0.09375, ((0, 8), (2, 4)))
    short_filter = gaussian(key_of[3], (3, 3, CH), 3 ** -0.5, 3.5, ((2, 4),), jnp.float32)
    long_filter = gaussian(key_of[4], (GROUPS_WIN, FLEN), FLEN ** -0.5, 0.5, ((0, 4),))
    skip_gain = gaussian(key_of[5], (CH,), 1.0, 4.0, ((0, 4),), jnp.float32)
    out_weight = gaussian(key_of[6], (CH, D), CH ** -0.5, 0.09375, ((0, 4), (1, 8)))
    return {"tokens": tokens, "norm_gain": norm_gain, "in_weight": in_weight, "short_filter": short_filter, "long_filter": long_filter, "skip_gain": skip_gain, "out_weight": out_weight}


def reference(tokens, norm_gain, in_weight, short_filter, long_filter, skip_gain, out_weight):
    filters = jnp.repeat(long_filter, GROUP, axis=0).astype(jnp.float32)
    values = tokens.astype(jnp.float32)
    mean_square = lax.optimization_barrier(jnp.mean(values * values, axis=-1, keepdims=True))
    normed = (values * lax.rsqrt(mean_square + 1e-06) * norm_gain).astype(jnp.bfloat16)
    proj = jnp.dot(normed, in_weight.reshape(D, 3 * CH), preferred_element_type=jnp.float32).astype(jnp.bfloat16)
    projf = proj.astype(jnp.float32).reshape(SEQ, 3, CH)
    padded = jnp.pad(projf, ((2, 0), (0, 0), (0, 0)))
    filtered = short_filter[0] * projf + short_filter[1] * padded[1:-1] + short_filter[2] * padded[:-2]
    out_gate = filtered[:, 0]
    key_part = filtered[:, 1]
    value_part = filtered[:, 2]
    product = (key_part * value_part).astype(jnp.bfloat16)
    prodf = product.astype(jnp.float32)
    extended = jnp.concatenate([jnp.zeros((FLEN - 1, CH), jnp.float32), prodf], axis=0)

    def add_tap(tap_index, accum):
        shifted = lax.dynamic_slice_in_dim(extended, (FLEN - 1 - tap_index).astype(jnp.int32), SEQ, 0)
        return accum + filters[:, tap_index] * shifted
    conv = lax.fori_loop(0, FLEN, add_tap, jnp.zeros((SEQ, CH), jnp.float32))
    gated = (out_gate * (conv + skip_gain * prodf)).astype(jnp.bfloat16)
    return jnp.dot(gated, out_weight, preferred_element_type=jnp.float32).astype(jnp.bfloat16)
```

```python
import functools

import jax
import jax.numpy as jnp
from jax import lax
from jax.experimental import pallas as pl
from jax.experimental.pallas import tpu as pltpu
from jax.sharding import PartitionSpec as P


def passed_along(block, axis, distance):
    devices = range(lax.axis_size(axis))
    route = [(i - distance, i) for i in devices if i - distance in devices]
    return lax.ppermute(block, axis, route)


def toeplitz_blocks(long_filter, row_count):
    groups = long_filter.shape[0]
    flen = long_filter.shape[1]
    window = flen + row_count - 1
    reversed_taps = long_filter[:, ::-1]
    padded = jnp.concatenate(
        [reversed_taps, jnp.zeros((groups, row_count), long_filter.dtype)], axis=1
    )
    tiled = jnp.tile(padded, (1, row_count))
    return tiled[:, : row_count * window].reshape(groups, row_count, window)


def short_conv(taps, extended):
    return taps[0] * extended[2:] + taps[1] * extended[1:-1] + taps[2] * extended[:-2]


def slab_plan(tokens, norm_gain, in_weight, short_filter, long_filter, skip_gain, out_weight):
    whole = lax.all_gather(tokens, "fsdp", axis=1, tiled=True)
    row_count = whole.shape[0]
    values = whole.astype(jnp.float32)
    mean_square = jnp.mean(values * values, axis=-1, keepdims=True)
    normed = (values * lax.rsqrt(mean_square + 1e-06) * norm_gain).astype(jnp.bfloat16)
    share = in_weight.shape[2]
    width_all = 3 * share
    weight_rows = lax.all_gather(in_weight, "ctx", axis=0, tiled=True)
    flat_rows = weight_rows.reshape(weight_rows.shape[0], width_all)
    proj = jnp.dot(normed, flat_rows, preferred_element_type=jnp.float32).astype(jnp.bfloat16)
    taps = short_filter.reshape(3, width_all)
    flen = long_filter.shape[1]
    earlier = passed_along(proj[row_count - 2 :], "ctx", 1)
    extended = jnp.concatenate([earlier, proj], axis=0).astype(jnp.float32)
    filtered = short_conv(taps, extended)
    out_gate = filtered[:, :share]
    product = (filtered[:, share : 2 * share] * filtered[:, 2 * share :]).astype(jnp.bfloat16)
    previous = passed_along(product[row_count - (flen - 1) :], "ctx", 1)
    product_ext = jnp.concatenate([previous, product], axis=0)
    groups = long_filter.shape[0]
    group_width = share // groups
    window = row_count + flen - 1
    blocks = toeplitz_blocks(long_filter, row_count)
    conv = jnp.einsum(
        "gts,sgc->tgc",
        blocks,
        product_ext.reshape(window, groups, group_width),
        preferred_element_type=jnp.float32,
    ).reshape(row_count, share)
    gated = (out_gate * (conv + skip_gain * product.astype(jnp.float32))).astype(jnp.bfloat16)
    terms = jnp.dot(
        gated,
        lax.all_gather(out_weight, "ctx", axis=1, tiled=True),
        preferred_element_type=jnp.float32,
    )
    mixed = lax.psum_scatter(terms, "fsdp", scatter_dimension=1, tiled=True).astype(jnp.bfloat16)
    return mixed


MESH = pl.DeviceIdType.MESH
LANE = 128


def meet(peers):
    barrier = pltpu.get_barrier_semaphore()
    for peer in peers:
        pl.semaphore_signal(barrier, inc=1, device_id=peer, device_id_type=MESH)
    pl.semaphore_wait(barrier, len(peers))


class Relay:
    def __init__(self, own, place, sends, recvs, across):
        self.me = (lax.axis_index("ctx"), lax.axis_index("fsdp"))
        self.line = lax.axis_size("ctx") // 2
        self.width = lax.axis_size("fsdp")
        self.high, self.low = self.me[0] // 2, self.me[0] % 2
        self.own, self.place = own, place
        self.sends, self.recvs = sends, recvs
        self.across = across

    def copy(self, kind, block, target, own=False):
        index = block[0] * self.width + block[1]
        return pltpu.make_async_remote_copy(
            src_ref=self.own if own else self.place(*block),
            dst_ref=self.place(*block),
            send_sem=self.sends.at[kind, index],
            recv_sem=self.recvs.at[index],
            device_id=target,
            device_id_type=MESH,
        )

    def visit(self, kind, block, own, action):
        ctx, fsdp = self.me
        if kind == 0:
            @pl.when(self.high < self.line - 1)
            def _():
                action(self.copy(0, block, (ctx + 2, fsdp), own))
        elif kind == 1:
            @pl.when(self.high > 0)
            def _():
                action(self.copy(1, block, (ctx - 2, fsdp), own))
        elif kind == 2:
            action(self.copy(2, block, (ctx + 1 - 2 * self.low, fsdp), own))
        elif kind == 3:
            x, core = fsdp // 2, fsdp % 2
            action(self.copy(3, block, (ctx, (1 - x) * 2 + core), own))
        else:
            action(self.copy(4, block, (ctx, fsdp + 1 - 2 * (fsdp % 2)), own))

    def arrive(self, block):
        self.copy(0, block, (self.me[0], self.me[1])).wait_recv()

    def run(self, action, landed, after_first=None):
        ctx, fsdp = self.me
        high, low = self.high, self.low
        for kind in (0, 1, 2) + self.across:
            self.visit(kind, (ctx, fsdp), True, action)
        for away in range(self.line + 1):
            if 1 <= away < self.line:
                @pl.when(high >= away)
                def _():
                    block = ((high - away) * 2 + low, fsdp)
                    landed(block)
                    for kind in (0, 2) + self.across:
                        self.visit(kind, block, False, action)

                @pl.when(high + away < self.line)
                def _():
                    block = ((high + away) * 2 + low, fsdp)
                    landed(block)
                    for kind in (1, 2) + self.across:
                        self.visit(kind, block, False, action)
            if away == 1 and after_first is not None:
                after_first()
            if away >= 1:
                back = away - 1
                for sign in (-1, 1) if back else (1,):
                    at = high + sign * back

                    @pl.when((at >= 0) & (at < self.line))
                    def _():
                        block = (at * 2 + 1 - low, fsdp)
                        landed(block)
                        for kind in self.across:
                            self.visit(kind, block, False, action)
        if 3 in self.across:
            other = (1 - fsdp // 2) * 2 + fsdp % 2
            for step in range(2 * self.line):
                block = ((ctx + step) % (2 * self.line), other)
                landed(block)
                self.visit(4, block, False, action)
            for step in range(2 * self.line):
                for x in range(2):
                    landed(((ctx + step) % (2 * self.line), x * 2 + 1 - fsdp % 2))

    def go(self, after_first=None):
        self.run(lambda copy: copy.start(), self.arrive, after_first)

    def finish(self):
        self.run(lambda copy: copy.wait_send(), lambda block: None)


def spread_kernel(rows_ref, weight_ref, all_ref, mine_ref, sends, recvs, w_sends, w_recvs, local):
    ctx, fsdp = lax.axis_index("ctx"), lax.axis_index("fsdp")
    slabs = lax.axis_size("ctx")
    rows, features = rows_ref.shape
    others = [((ctx + step) % slabs, fsdp) for step in range(1, slabs)]
    x, core = fsdp // 2, fsdp % 2
    meet(others + [(ctx, (1 - x) * 2 + core), (ctx, x * 2 + 1 - core)])

    def place(slab, part):
        return all_ref.at[pl.ds(slab * rows, rows), pl.ds(part * features, features)]

    own = [
        pltpu.make_async_copy(rows_ref, place(ctx, fsdp), local.at[0]),
        pltpu.make_async_copy(weight_ref.at[ctx], mine_ref.at[ctx], local.at[1]),
    ]

    def weight_copy(step):
        target = (ctx + step) % slabs
        return pltpu.make_async_remote_copy(
            src_ref=weight_ref.at[target],
            dst_ref=mine_ref.at[ctx],
            send_sem=w_sends.at[step],
            recv_sem=w_recvs.at[step],
            device_id=(target, fsdp),
            device_id_type=MESH,
        )

    def send_weights():
        for step in range(1, slabs):
            weight_copy(step).start()

    relay = Relay(rows_ref, place, sends, recvs, (3, 4))
    for copy in own:
        copy.start()
    relay.go(send_weights)
    for step in range(1, slabs):
        source = (ctx + slabs - step) % slabs
        pltpu.make_async_remote_copy(
            src_ref=weight_ref.at[source],
            dst_ref=mine_ref.at[source],
            send_sem=w_sends.at[step],
            recv_sem=w_recvs.at[step],
            device_id=(source, fsdp),
            device_id_type=MESH,
        ).wait_recv()
    relay.finish()
    for step in range(1, slabs):
        weight_copy(step).wait_send()
    for copy in own:
        copy.wait()


def collect_kernel(cols_ref, all_ref, sends, recvs, local):
    ctx, fsdp = lax.axis_index("ctx"), lax.axis_index("fsdp")
    slabs = lax.axis_size("ctx")
    width = cols_ref.shape[1]
    meet([((ctx + step) % slabs, fsdp) for step in range(1, slabs)])

    def place(slab, part):
        return all_ref.at[:, pl.ds(slab * width, width)]

    own = pltpu.make_async_copy(cols_ref, place(ctx, fsdp), local.at[0])
    own.start()
    relay = Relay(cols_ref, place, sends, recvs, ())
    relay.go()
    relay.finish()
    own.wait()


def deliver_kernel(terms_ref, out_ref, sends, recvs, local):
    ctx, fsdp = lax.axis_index("ctx"), lax.axis_index("fsdp")
    slabs, parts = lax.axis_size("ctx"), lax.axis_size("fsdp")
    fold = slabs // parts
    width = terms_ref.shape[2]
    home = ctx // fold
    mixed_in = home == fsdp

    barrier = pltpu.get_barrier_semaphore()
    for slab in range(slabs):
        @pl.when(jnp.logical_not(mixed_in & (slab == ctx)))
        def _():
            pl.semaphore_signal(barrier, inc=1, device_id=(slab, home), device_id_type=MESH)

    for part in range(parts):
        for half in range(fold):
            source = fsdp * fold + half

            @pl.when(jnp.logical_not((part == fsdp) & (source == ctx)))
            def _():
                pl.semaphore_signal(barrier, inc=1, device_id=(source, part), device_id_type=MESH)

    @pl.when(mixed_in)
    def _():
        pl.semaphore_wait(barrier, slabs + parts * fold - 2)

    @pl.when(jnp.logical_not(mixed_in))
    def _():
        pl.semaphore_wait(barrier, slabs + parts * fold)

    def slot(part, source):
        return out_ref.at[part, :, pl.ds((source % fold) * width, width)]

    def outgoing(slab):
        return pltpu.make_async_remote_copy(
            src_ref=terms_ref.at[slab],
            dst_ref=slot(fsdp, ctx),
            send_sem=sends.at[slab],
            recv_sem=recvs.at[fsdp * fold + ctx % fold],
            device_id=(slab, home),
            device_id_type=MESH,
        )

    def each(action):
        for step in range(slabs):
            slab = (ctx + step) % slabs

            @pl.when(jnp.logical_not(mixed_in & (slab == ctx)))
            def _():
                action(slab)

    own = pltpu.make_async_copy(terms_ref.at[ctx], slot(fsdp, ctx), local.at[0])
    each(lambda slab: outgoing(slab).start())

    @pl.when(mixed_in)
    def _():
        own.start()

    for part in range(parts):
        for half in range(fold):
            source = fsdp * fold + half

            @pl.when(jnp.logical_not((part == fsdp) & (source == ctx)))
            def _():
                pltpu.make_async_remote_copy(
                    src_ref=terms_ref.at[0],
                    dst_ref=slot(part, source),
                    send_sem=sends.at[0],
                    recv_sem=recvs.at[part * fold + half],
                    device_id=(source, part),
                    device_id_type=MESH,
                ).wait_recv()

    each(lambda slab: outgoing(slab).wait_send())

    @pl.when(mixed_in)
    def _():
        own.wait()


VMEM_SPEC = pl.BlockSpec(memory_space=pltpu.VMEM)
ANY_SPEC = pl.BlockSpec(memory_space=pl.ANY)
DMA = pltpu.SemaphoreType.DMA


def params(number):
    return pltpu.CompilerParams(collective_id=number, has_side_effects=True)


def spread(rows, weights):
    slabs, parts = lax.axis_size("ctx"), lax.axis_size("fsdp")
    return pl.pallas_call(
        spread_kernel,
        out_shape=(
            jax.ShapeDtypeStruct((rows.shape[0] * slabs, rows.shape[1] * parts), rows.dtype),
            jax.ShapeDtypeStruct(weights.shape, weights.dtype),
        ),
        in_specs=[VMEM_SPEC, VMEM_SPEC],
        out_specs=(ANY_SPEC, ANY_SPEC),
        scratch_shapes=[
            DMA((5, slabs * parts)), DMA((slabs * parts,)), DMA((slabs,)), DMA((slabs,)), DMA((2,)),
        ],
        compiler_params=params(0),
    )(rows, weights)


def collect(cols):
    slabs, parts = lax.axis_size("ctx"), lax.axis_size("fsdp")
    return pl.pallas_call(
        collect_kernel,
        out_shape=jax.ShapeDtypeStruct((cols.shape[0], cols.shape[1] * slabs), cols.dtype),
        in_specs=[VMEM_SPEC],
        out_specs=ANY_SPEC,
        scratch_shapes=[DMA((3, slabs * parts)), DMA((slabs * parts,)), DMA((1,))],
        compiler_params=params(1),
    )(cols)


def deliver(terms):
    slabs, parts = lax.axis_size("ctx"), lax.axis_size("fsdp")
    fold = slabs // parts
    return pl.pallas_call(
        deliver_kernel,
        out_shape=jax.ShapeDtypeStruct((parts, terms.shape[1], terms.shape[2] * fold), terms.dtype),
        in_specs=[VMEM_SPEC],
        out_specs=ANY_SPEC,
        scratch_shapes=[DMA((slabs,)), DMA((parts * fold,)), DMA((1,))],
        compiler_params=params(2),
    )(terms)


def channel_plan(tokens, norm_gain, in_weight, short_filter, long_filter, skip_gain, out_weight):
    ctx, fsdp = lax.axis_index("ctx"), lax.axis_index("fsdp")
    slabs, parts = lax.axis_size("ctx"), lax.axis_size("fsdp")
    rows, features = tokens.shape
    positions = rows * slabs
    share = in_weight.shape[2]
    own = share // slabs
    values = tokens.astype(jnp.float32)
    mean_square = lax.psum(jnp.sum(values * values, axis=-1, keepdims=True), "fsdp") / (features * parts)
    gain = lax.dynamic_slice_in_dim(norm_gain, fsdp * features, features, 0)
    normed = (values * lax.rsqrt(mean_square + 1e-06) * gain).astype(jnp.bfloat16)

    pieces = in_weight.reshape(in_weight.shape[0], 3, slabs, own).transpose(2, 0, 1, 3)
    pieces = pieces.reshape(slabs, in_weight.shape[0], 3 * own)
    whole, weights = spread(normed, pieces)
    weights = weights.reshape(slabs * in_weight.shape[0], 3 * own)
    proj = jnp.dot(whole, weights, preferred_element_type=jnp.float32).astype(jnp.bfloat16)

    taps = lax.dynamic_slice_in_dim(short_filter, ctx * own, own, 2).reshape(3, 3 * own)
    extended = jnp.pad(proj.astype(jnp.float32), ((2, 0), (0, 0)))
    filtered = short_conv(taps, extended)
    product = (filtered[:, own : 2 * own] * filtered[:, 2 * own :]).astype(jnp.bfloat16)

    flen = long_filter.shape[1]
    group_count = long_filter.shape[0] // slabs
    group_width = own // group_count
    filters = lax.dynamic_slice_in_dim(long_filter, ctx * group_count, group_count, 0)
    blocks = jnp.pad(toeplitz_blocks(filters, flen), ((0, 0), (0, 0), (1, 0)))
    count = positions // flen
    tiles = product.reshape(count, flen, group_count, group_width)
    before = jnp.pad(tiles, ((1, 0), (0, 0), (0, 0), (0, 0)))[:-1]
    windows = jnp.concatenate([before, tiles], axis=1)
    conv = jnp.einsum("gts,bsgc->btgc", blocks, windows, preferred_element_type=jnp.float32)
    conv = conv.reshape(positions, own)
    skip = lax.dynamic_slice_in_dim(skip_gain, ctx * own, own, 0)
    gated = (filtered[:, :own] * (conv + skip * product.astype(jnp.float32))).astype(jnp.bfloat16)

    terms = jnp.dot(collect(gated), out_weight, preferred_element_type=jnp.float32)
    terms = terms.astype(jnp.bfloat16).reshape(slabs, rows, out_weight.shape[1])
    arrived = deliver(terms)
    return jnp.sum(arrived.astype(jnp.float32), axis=0).astype(jnp.bfloat16)


def on_device(tokens, *rest):
    slabs, parts = lax.axis_size("ctx"), lax.axis_size("fsdp")
    own = rest[1].shape[2] // slabs
    gathered = tokens.size * slabs * parts * 2
    fits = parts == 4 and slabs % parts == 0 and own % LANE == 0 and gathered <= 2**25
    return (channel_plan if fits else slab_plan)(tokens, *rest)


def solution(mesh):
    in_specs = (
        P("ctx", "fsdp"),
        P(),
        P("ctx", None, "fsdp"),
        P(None, None, "fsdp"),
        P("fsdp", None),
        P("fsdp"),
        P("fsdp", "ctx"),
    )
    out_specs = P("ctx", "fsdp")
    return jax.shard_map(
        on_device, mesh=mesh, in_specs=in_specs, out_specs=out_specs, check_vma=False
    )
```

```python
import functools

import jax
import jax.numpy as jnp
from jax import lax
from jax.experimental import pallas as pl
from jax.experimental.pallas import tpu as pltpu
from jax.sharding import PartitionSpec as P


def passed_along(block, axis, distance):
    devices = range(lax.axis_size(axis))
    route = [(i - distance, i) for i in devices if i - distance in devices]
    return lax.ppermute(block, axis, route)


def toeplitz_blocks(long_filter, row_count):
    groups = long_filter.shape[0]
    flen = long_filter.shape[1]
    window = flen + row_count - 1
    reversed_taps = long_filter[:, ::-1]
    padded = jnp.concatenate(
        [reversed_taps, jnp.zeros((groups, row_count), long_filter.dtype)], axis=1
    )
    tiled = jnp.tile(padded, (1, row_count))
    return tiled[:, : row_count * window].reshape(groups, row_count, window)


def short_conv(taps, extended):
    return taps[0] * extended[2:] + taps[1] * extended[1:-1] + taps[2] * extended[:-2]


def slab_plan(tokens, norm_gain, in_weight, short_filter, long_filter, skip_gain, out_weight):
    whole = lax.all_gather(tokens, "fsdp", axis=1, tiled=True)
    row_count = whole.shape[0]
    values = whole.astype(jnp.float32)
    mean_square = jnp.mean(values * values, axis=-1, keepdims=True)
    normed = (values * lax.rsqrt(mean_square + 1e-06) * norm_gain).astype(jnp.bfloat16)
    share = in_weight.shape[2]
    width_all = 3 * share
    weight_rows = lax.all_gather(in_weight, "ctx", axis=0, tiled=True)
    flat_rows = weight_rows.reshape(weight_rows.shape[0], width_all)
    proj = jnp.dot(normed, flat_rows, preferred_element_type=jnp.float32).astype(jnp.bfloat16)
    taps = short_filter.reshape(3, width_all)
    flen = long_filter.shape[1]
    earlier = passed_along(proj[row_count - 2 :], "ctx", 1)
    extended = jnp.concatenate([earlier, proj], axis=0).astype(jnp.float32)
    filtered = short_conv(taps, extended)
    out_gate = filtered[:, :share]
    product = (filtered[:, share : 2 * share] * filtered[:, 2 * share :]).astype(jnp.bfloat16)
    previous = passed_along(product[row_count - (flen - 1) :], "ctx", 1)
    product_ext = jnp.concatenate([previous, product], axis=0)
    groups = long_filter.shape[0]
    group_width = share // groups
    window = row_count + flen - 1
    blocks = toeplitz_blocks(long_filter, row_count)
    conv = jnp.einsum(
        "gts,sgc->tgc",
        blocks,
        product_ext.reshape(window, groups, group_width),
        preferred_element_type=jnp.float32,
    ).reshape(row_count, share)
    gated = (out_gate * (conv + skip_gain * product.astype(jnp.float32))).astype(jnp.bfloat16)
    terms = jnp.dot(
        gated,
        lax.all_gather(out_weight, "ctx", axis=1, tiled=True),
        preferred_element_type=jnp.float32,
    )
    mixed = lax.psum_scatter(terms, "fsdp", scatter_dimension=1, tiled=True).astype(jnp.bfloat16)
    return mixed


MESH = pl.DeviceIdType.MESH
LANE = 128


def meet(peers):
    barrier = pltpu.get_barrier_semaphore()
    for peer in peers:
        pl.semaphore_signal(barrier, inc=1, device_id=peer, device_id_type=MESH)
    pl.semaphore_wait(barrier, len(peers))


class Relay:
    def __init__(self, own, place, sends, recvs, across, half=None):
        self.me = (lax.axis_index("ctx"), lax.axis_index("fsdp"))
        self.line = lax.axis_size("ctx") // 2
        self.width = lax.axis_size("fsdp")
        self.high, self.low = self.me[0] // 2, self.me[0] % 2
        self.own, self.place = own, place
        self.sends, self.recvs = sends, recvs
        self.across = across
        self.half = half

    def copy(self, kind, block, target, own=False):
        index = block[0] * self.width + block[1]
        return pltpu.make_async_remote_copy(
            src_ref=self.own if own else self.place(*block),
            dst_ref=self.place(*block),
            send_sem=self.sends.at[kind, index],
            recv_sem=self.recvs.at[index],
            device_id=target,
            device_id_type=MESH,
        )

    def visit(self, kind, block, own, action):
        ctx, fsdp = self.me
        if kind == 0:
            @pl.when(self.high < self.line - 1)
            def _():
                action(self.copy(0, block, (ctx + 2, fsdp), own))
        elif kind == 1:
            @pl.when(self.high > 0)
            def _():
                action(self.copy(1, block, (ctx - 2, fsdp), own))
        elif kind == 2:
            action(self.copy(2, block, (ctx + 1 - 2 * self.low, fsdp), own))
        elif kind == 3:
            x, core = fsdp // 2, fsdp % 2
            action(self.copy(3, block, (ctx, (1 - x) * 2 + core), own))
        elif self.half is not None:
            action(self.half(block, own))
        else:
            action(self.copy(4, block, (ctx, fsdp + 1 - 2 * (fsdp % 2)), own))

    def arrive(self, block):
        self.copy(0, block, (self.me[0], self.me[1])).wait_recv()

    def run(self, action, landed, after_first=None):
        ctx, fsdp = self.me
        high, low = self.high, self.low
        for kind in (0, 1, 2) + self.across:
            self.visit(kind, (ctx, fsdp), True, action)
        for away in range(self.line + 1):
            if 1 <= away < self.line:
                @pl.when(high >= away)
                def _():
                    block = ((high - away) * 2 + low, fsdp)
                    landed(block)
                    for kind in (0, 2) + self.across:
                        self.visit(kind, block, False, action)

                @pl.when(high + away < self.line)
                def _():
                    block = ((high + away) * 2 + low, fsdp)
                    landed(block)
                    for kind in (1, 2) + self.across:
                        self.visit(kind, block, False, action)
            if away == 1 and after_first is not None:
                after_first()
            if away >= 1:
                back = away - 1
                for sign in (-1, 1) if back else (1,):
                    at = high + sign * back

                    @pl.when((at >= 0) & (at < self.line))
                    def _():
                        block = (at * 2 + 1 - low, fsdp)
                        landed(block)
                        for kind in self.across:
                            self.visit(kind, block, False, action)
        if 3 in self.across:
            other = (1 - fsdp // 2) * 2 + fsdp % 2
            for step in range(2 * self.line):
                block = ((ctx + step) % (2 * self.line), other)
                landed(block)
                self.visit(4, block, False, action)
            for step in range(2 * self.line):
                for x in range(2):
                    landed(((ctx + step) % (2 * self.line), x * 2 + 1 - fsdp % 2))

    def go(self, after_first=None):
        self.run(lambda copy: copy.start(), self.arrive, after_first)

    def finish(self):
        self.run(lambda copy: copy.wait_send(), lambda block: None)


def spread_kernel(
    rows_ref, weight_ref, out_ref, all_ref, mine_ref, theirs_ref,
    sends, recvs, w_sends, w_recvs, o_sems, local,
):
    ctx, fsdp = lax.axis_index("ctx"), lax.axis_index("fsdp")
    slabs = lax.axis_size("ctx")
    rows, features = rows_ref.shape
    kinds, depth, share = weight_ref.shape
    width = share // slabs
    others = [((ctx + step) % slabs, fsdp) for step in range(1, slabs)]
    x, core = fsdp // 2, fsdp % 2
    meet(others + [(ctx, (1 - x) * 2 + core), (ctx, x * 2 + 1 - core)])

    def place(slab, part):
        return all_ref.at[pl.ds(slab * rows, rows), pl.ds(part * features, features)]

    def piece(kind, slab):
        return weight_ref.at[kind, :, pl.ds(slab * width, width)]

    def landing(kind, slab):
        return mine_ref.at[pl.ds(slab * depth, depth), pl.ds(kind * width, width)]

    own = [pltpu.make_async_copy(rows_ref, place(ctx, fsdp), local.at[0])] + [
        pltpu.make_async_copy(piece(kind, ctx), landing(kind, ctx), local.at[1 + kind])
        for kind in range(kinds)
    ]

    def weight_copies(step, away):
        return [
            pltpu.make_async_remote_copy(
                src_ref=piece(kind, away),
                dst_ref=landing(kind, ctx),
                send_sem=w_sends.at[step, kind],
                recv_sem=w_recvs.at[step, kind],
                device_id=(away, fsdp),
                device_id_type=MESH,
            )
            for kind in range(kinds)
        ]

    def arrived_weights(step):
        source = (ctx + slabs - step) % slabs
        for kind in range(kinds):
            pltpu.make_async_remote_copy(
                src_ref=piece(kind, source),
                dst_ref=landing(kind, source),
                send_sem=w_sends.at[step, kind],
                recv_sem=w_recvs.at[step, kind],
                device_id=(source, fsdp),
                device_id_type=MESH,
            ).wait_recv()

    def send_weights():
        for step in range(1, slabs):
            for copy in weight_copies(step, (ctx + step) % slabs):
                copy.start()

    swap = pltpu.make_async_remote_copy(
        src_ref=out_ref,
        dst_ref=theirs_ref,
        send_sem=o_sems.at[0],
        recv_sem=o_sems.at[1],
        device_id=(ctx, x * 2 + 1 - core),
        device_id_type=MESH,
    )
    relay = Relay(rows_ref, place, sends, recvs, (3, 4))
    for copy in own:
        copy.start()
    swap.start()
    relay.go(send_weights)
    for step in range(1, slabs):
        arrived_weights(step)
    relay.finish()
    for step in range(1, slabs):
        for copy in weight_copies(step, (ctx + step) % slabs):
            copy.wait_send()
    swap.wait()
    for copy in own:
        copy.wait()


def collect_kernel(cols_ref, all_ref, other_ref, sends, recvs, half_recvs, local):
    ctx, fsdp = lax.axis_index("ctx"), lax.axis_index("fsdp")
    slabs, parts = lax.axis_size("ctx"), lax.axis_size("fsdp")
    width = cols_ref.shape[2]
    x, core = fsdp // 2, fsdp % 2
    partner = (ctx, x * 2 + 1 - core)
    meet([((ctx + step) % slabs, fsdp) for step in range(1, slabs)] + [partner])

    def place(slab, part):
        return all_ref.at[:, :, pl.ds(slab * width, width)]

    def half(block, own):
        cols = pl.ds(block[0] * width, width)
        return pltpu.make_async_remote_copy(
            src_ref=cols_ref.at[1 - core] if own else all_ref.at[1 - core, :, cols],
            dst_ref=other_ref.at[:, cols],
            send_sem=sends.at[3, block[0] * parts + fsdp],
            recv_sem=half_recvs.at[block[0]],
            device_id=partner,
            device_id_type=MESH,
        )

    own = pltpu.make_async_copy(cols_ref, place(ctx, fsdp), local.at[0])
    own.start()
    relay = Relay(cols_ref, place, sends, recvs, (4,), half)
    relay.go()
    for step in range(slabs):
        half(((ctx + step) % slabs, fsdp), False).wait_recv()
    relay.finish()
    own.wait()


def deliver_kernel(terms_ref, out_ref, sends, recvs, local):
    ctx, fsdp = lax.axis_index("ctx"), lax.axis_index("fsdp")
    slabs, parts = lax.axis_size("ctx"), lax.axis_size("fsdp")
    fold = slabs // parts
    width = terms_ref.shape[2]
    x, core = fsdp // 2, fsdp % 2
    home = ctx // fold
    stays = (home == fsdp) & (ctx % 2 == core)
    targets = [(ctx // 2 + step) % (slabs // 2) for step in range(slabs // 2)]
    sources = [(half, other) for half in range(fold) for other in range(parts // 2)]

    def to_others(action):
        for high in targets:
            @pl.when(jnp.logical_not(stays & (high == ctx // 2)))
            def _():
                action(high, (high * 2 + core, home))

    def from_others(action):
        for half, other in sources:
            source = (fsdp * fold + half, other * 2 + ctx % 2)

            @pl.when(jnp.logical_not((source[0] == ctx) & (source[1] == fsdp)))
            def _():
                action(half, other, source)

    barrier = pltpu.get_barrier_semaphore()

    def greet(device):
        pl.semaphore_signal(barrier, inc=1, device_id=device, device_id_type=MESH)

    to_others(lambda high, device: greet(device))
    from_others(lambda half, other, device: greet(device))

    @pl.when(stays)
    def _():
        pl.semaphore_wait(barrier, len(targets) + len(sources) - 2)

    @pl.when(jnp.logical_not(stays))
    def _():
        pl.semaphore_wait(barrier, len(targets) + len(sources))

    def slot(half, other):
        return out_ref.at[other, :, pl.ds(half * width, width)]

    def outgoing(high, device):
        return pltpu.make_async_remote_copy(
            src_ref=terms_ref.at[high],
            dst_ref=slot(ctx % fold, x),
            send_sem=sends.at[high],
            recv_sem=recvs.at[x * fold + ctx % fold],
            device_id=device,
            device_id_type=MESH,
        )

    def incoming(half, other, device):
        return pltpu.make_async_remote_copy(
            src_ref=terms_ref.at[0],
            dst_ref=slot(half, other),
            send_sem=sends.at[0],
            recv_sem=recvs.at[other * fold + half],
            device_id=device,
            device_id_type=MESH,
        )

    own = pltpu.make_async_copy(terms_ref.at[ctx // 2], slot(ctx % fold, x), local.at[0])
    to_others(lambda high, device: outgoing(high, device).start())

    @pl.when(stays)
    def _():
        own.start()

    from_others(lambda half, other, device: incoming(half, other, device).wait_recv())
    to_others(lambda high, device: outgoing(high, device).wait_send())

    @pl.when(stays)
    def _():
        own.wait()


VMEM_SPEC = pl.BlockSpec(memory_space=pltpu.VMEM)
ANY_SPEC = pl.BlockSpec(memory_space=pl.ANY)
DMA = pltpu.SemaphoreType.DMA


def params(number):
    return pltpu.CompilerParams(collective_id=number, has_side_effects=True)


def spread(rows, weights, out_weight):
    slabs, parts = lax.axis_size("ctx"), lax.axis_size("fsdp")
    kinds, depth, share = weights.shape
    return pl.pallas_call(
        spread_kernel,
        out_shape=(
            jax.ShapeDtypeStruct((rows.shape[0] * slabs, rows.shape[1] * parts), rows.dtype),
            jax.ShapeDtypeStruct((depth * slabs, kinds * share // slabs), weights.dtype),
            jax.ShapeDtypeStruct(out_weight.shape, out_weight.dtype),
        ),
        in_specs=[VMEM_SPEC, VMEM_SPEC, VMEM_SPEC],
        out_specs=(ANY_SPEC, ANY_SPEC, ANY_SPEC),
        scratch_shapes=[
            DMA((5, slabs * parts)), DMA((slabs * parts,)),
            DMA((slabs, kinds)), DMA((slabs, kinds)), DMA((2,)), DMA((1 + kinds,)),
        ],
        compiler_params=params(0),
    )(rows, weights, out_weight)


def collect(cols):
    slabs, parts = lax.axis_size("ctx"), lax.axis_size("fsdp")
    halves, rows, width = cols.shape
    return pl.pallas_call(
        collect_kernel,
        out_shape=(
            jax.ShapeDtypeStruct((halves, rows, width * slabs), cols.dtype),
            jax.ShapeDtypeStruct((rows, width * slabs), cols.dtype),
        ),
        in_specs=[VMEM_SPEC],
        out_specs=(ANY_SPEC, ANY_SPEC),
        scratch_shapes=[DMA((5, slabs * parts)), DMA((slabs * parts,)), DMA((slabs,)), DMA((1,))],
        compiler_params=params(1),
    )(cols)


def deliver(terms):
    slabs, parts = lax.axis_size("ctx"), lax.axis_size("fsdp")
    fold = slabs // parts
    return pl.pallas_call(
        deliver_kernel,
        out_shape=jax.ShapeDtypeStruct((parts // 2, terms.shape[1], terms.shape[2] * fold), terms.dtype),
        in_specs=[VMEM_SPEC],
        out_specs=ANY_SPEC,
        scratch_shapes=[DMA((slabs // 2,)), DMA((fold * parts // 2,)), DMA((1,))],
        compiler_params=params(2),
    )(terms)


def channel_plan(tokens, norm_gain, in_weight, short_filter, long_filter, skip_gain, out_weight):
    ctx, fsdp = lax.axis_index("ctx"), lax.axis_index("fsdp")
    slabs, parts = lax.axis_size("ctx"), lax.axis_size("fsdp")
    rows, features = tokens.shape
    positions = rows * slabs
    share = in_weight.shape[2]
    own = share // slabs
    values = tokens.astype(jnp.float32)
    mean_square = lax.psum(jnp.sum(values * values, axis=-1, keepdims=True), "fsdp") / (features * parts)
    gain = lax.dynamic_slice_in_dim(norm_gain, fsdp * features, features, 0)
    normed = (values * lax.rsqrt(mean_square + 1e-06) * gain).astype(jnp.bfloat16)

    whole, weights, partner_weight = spread(normed, in_weight.transpose(1, 0, 2), out_weight)
    proj = jnp.dot(whole, weights, preferred_element_type=jnp.float32)
    proj = lax.reduce_precision(proj, 8, 7).astype(jnp.bfloat16)

    taps = lax.dynamic_slice_in_dim(short_filter, ctx * own, own, 2).reshape(3, 3 * own)
    extended = jnp.pad(proj.astype(jnp.float32), ((2, 0), (0, 0)))
    filtered = short_conv(taps, extended)
    product = filtered[:, own : 2 * own] * filtered[:, 2 * own :]
    product = lax.reduce_precision(product, 8, 7).astype(jnp.bfloat16)

    flen = long_filter.shape[1]
    group_count = long_filter.shape[0] // slabs
    group_width = own // group_count
    filters = lax.dynamic_slice_in_dim(long_filter, ctx * group_count, group_count, 0)
    blocks = jnp.pad(toeplitz_blocks(filters, flen), ((0, 0), (0, 0), (1, 0)))
    count = positions // flen
    tiles = product.reshape(count, flen, group_count, group_width)
    before = jnp.pad(tiles, ((1, 0), (0, 0), (0, 0), (0, 0)))[:-1]
    windows = jnp.concatenate([before, tiles], axis=1)
    conv = jnp.einsum("gts,bsgc->btgc", blocks, windows, preferred_element_type=jnp.float32)
    conv = conv.reshape(positions, own)
    skip = lax.dynamic_slice_in_dim(skip_gain, ctx * own, own, 0)
    gated = (filtered[:, :own] * (conv + skip * product.astype(jnp.float32))).astype(jnp.bfloat16)

    by_core = gated.reshape(slabs // 2, 2, rows, own).transpose(1, 0, 2, 3)
    every, partner_cols = collect(by_core.reshape(2, positions // 2, own))
    core_cols = lax.dynamic_index_in_dim(every, fsdp % 2, 0, keepdims=False)
    terms = jnp.dot(core_cols, out_weight, preferred_element_type=jnp.float32)
    terms += jnp.dot(partner_cols, partner_weight, preferred_element_type=jnp.float32)
    terms = terms.astype(jnp.bfloat16).reshape(slabs // 2, rows, out_weight.shape[1])
    arrived = deliver(terms)
    return jnp.sum(arrived.astype(jnp.float32), axis=0).astype(jnp.bfloat16)


def on_device(tokens, *rest):
    slabs, parts = lax.axis_size("ctx"), lax.axis_size("fsdp")
    own = rest[1].shape[2] // slabs
    gathered = tokens.size * slabs * parts * 2
    fits = parts == 4 and slabs % parts == 0 and own % LANE == 0 and gathered <= 2**25
    return (channel_plan if fits else slab_plan)(tokens, *rest)


def solution(mesh):
    in_specs = (
        P("ctx", "fsdp"),
        P(),
        P("ctx", None, "fsdp"),
        P(None, None, "fsdp"),
        P("fsdp", None),
        P("fsdp"),
        P("fsdp", "ctx"),
    )
    out_specs = P("ctx", "fsdp")
    return jax.shard_map(
        on_device, mesh=mesh, in_specs=in_specs, out_specs=out_specs, check_vma=False
    )
```

```python
import functools

import jax
import jax.numpy as jnp
from jax import lax
from jax.experimental import pallas as pl
from jax.experimental.pallas import tpu as pltpu
from jax.sharding import PartitionSpec as P


def passed_along(block, axis, distance):
    devices = range(lax.axis_size(axis))
    route = [(i - distance, i) for i in devices if i - distance in devices]
    return lax.ppermute(block, axis, route)


def toeplitz_blocks(long_filter, row_count):
    groups = long_filter.shape[0]
    flen = long_filter.shape[1]
    window = flen + row_count - 1
    reversed_taps = long_filter[:, ::-1]
    padded = jnp.concatenate(
        [reversed_taps, jnp.zeros((groups, row_count), long_filter.dtype)], axis=1
    )
    tiled = jnp.tile(padded, (1, row_count))
    return tiled[:, : row_count * window].reshape(groups, row_count, window)


def short_conv(taps, extended):
    return taps[0] * extended[2:] + taps[1] * extended[1:-1] + taps[2] * extended[:-2]


def slab_plan(tokens, norm_gain, in_weight, short_filter, long_filter, skip_gain, out_weight):
    whole = lax.all_gather(tokens, "fsdp", axis=1, tiled=True)
    row_count = whole.shape[0]
    values = whole.astype(jnp.float32)
    mean_square = jnp.mean(values * values, axis=-1, keepdims=True)
    normed = (values * lax.rsqrt(mean_square + 1e-06) * norm_gain).astype(jnp.bfloat16)
    share = in_weight.shape[2]
    width_all = 3 * share
    weight_rows = lax.all_gather(in_weight, "ctx", axis=0, tiled=True)
    flat_rows = weight_rows.reshape(weight_rows.shape[0], width_all)
    proj = jnp.dot(normed, flat_rows, preferred_element_type=jnp.float32).astype(jnp.bfloat16)
    taps = short_filter.reshape(3, width_all)
    flen = long_filter.shape[1]
    earlier = passed_along(proj[row_count - 2 :], "ctx", 1)
    extended = jnp.concatenate([earlier, proj], axis=0).astype(jnp.float32)
    filtered = short_conv(taps, extended)
    out_gate = filtered[:, :share]
    product = (filtered[:, share : 2 * share] * filtered[:, 2 * share :]).astype(jnp.bfloat16)
    previous = passed_along(product[row_count - (flen - 1) :], "ctx", 1)
    product_ext = jnp.concatenate([previous, product], axis=0)
    groups = long_filter.shape[0]
    group_width = share // groups
    window = row_count + flen - 1
    blocks = toeplitz_blocks(long_filter, row_count)
    conv = jnp.einsum(
        "gts,sgc->tgc",
        blocks,
        product_ext.reshape(window, groups, group_width),
        preferred_element_type=jnp.float32,
    ).reshape(row_count, share)
    gated = (out_gate * (conv + skip_gain * product.astype(jnp.float32))).astype(jnp.bfloat16)
    terms = jnp.dot(
        gated,
        lax.all_gather(out_weight, "ctx", axis=1, tiled=True),
        preferred_element_type=jnp.float32,
    )
    mixed = lax.psum_scatter(terms, "fsdp", scatter_dimension=1, tiled=True).astype(jnp.bfloat16)
    return mixed


MESH = pl.DeviceIdType.MESH
LANE = 128


def meet(peers):
    barrier = pltpu.get_barrier_semaphore()
    for peer in peers:
        pl.semaphore_signal(barrier, inc=1, device_id=peer, device_id_type=MESH)
    pl.semaphore_wait(barrier, len(peers))


class Relay:
    def __init__(self, own, place, sends, recvs, across, half=None):
        self.me = (lax.axis_index("ctx"), lax.axis_index("fsdp"))
        self.line = lax.axis_size("ctx") // 2
        self.width = lax.axis_size("fsdp")
        self.high, self.low = self.me[0] // 2, self.me[0] % 2
        self.own, self.place = own, place
        self.sends, self.recvs = sends, recvs
        self.across = across
        self.half = half

    def copy(self, kind, block, target, own=False):
        index = block[0] * self.width + block[1]
        return pltpu.make_async_remote_copy(
            src_ref=self.own if own else self.place(*block),
            dst_ref=self.place(*block),
            send_sem=self.sends.at[kind, index],
            recv_sem=self.recvs.at[index],
            device_id=target,
            device_id_type=MESH,
        )

    def visit(self, kind, block, own, action):
        ctx, fsdp = self.me
        if kind == 0:
            @pl.when(self.high < self.line - 1)
            def _():
                action(self.copy(0, block, (ctx + 2, fsdp), own))
        elif kind == 1:
            @pl.when(self.high > 0)
            def _():
                action(self.copy(1, block, (ctx - 2, fsdp), own))
        elif kind == 2:
            action(self.copy(2, block, (ctx + 1 - 2 * self.low, fsdp), own))
        elif kind == 3:
            x, core = fsdp // 2, fsdp % 2
            action(self.copy(3, block, (ctx, (1 - x) * 2 + core), own))
        elif self.half is not None:
            action(self.half(block, own))
        else:
            action(self.copy(4, block, (ctx, fsdp + 1 - 2 * (fsdp % 2)), own))

    def arrive(self, block):
        self.copy(0, block, (self.me[0], self.me[1])).wait_recv()

    def run(self, action, landed, after_first=None):
        ctx, fsdp = self.me
        high, low = self.high, self.low
        for kind in (0, 1, 2) + self.across:
            self.visit(kind, (ctx, fsdp), True, action)
        for away in range(self.line + 1):
            if 1 <= away < self.line:
                @pl.when(high >= away)
                def _():
                    block = ((high - away) * 2 + low, fsdp)
                    landed(block)
                    for kind in (0, 2) + self.across:
                        self.visit(kind, block, False, action)

                @pl.when(high + away < self.line)
                def _():
                    block = ((high + away) * 2 + low, fsdp)
                    landed(block)
                    for kind in (1, 2) + self.across:
                        self.visit(kind, block, False, action)
            if away < self.line and after_first is not None:
                after_first(away)
            if away >= 1:
                back = away - 1
                for sign in (-1, 1) if back else (1,):
                    at = high + sign * back

                    @pl.when((at >= 0) & (at < self.line))
                    def _():
                        block = (at * 2 + 1 - low, fsdp)
                        landed(block)
                        for kind in self.across:
                            self.visit(kind, block, False, action)
        if 3 in self.across:
            other = (1 - fsdp // 2) * 2 + fsdp % 2
            for step in range(2 * self.line):
                block = ((ctx + step) % (2 * self.line), other)
                landed(block)
                self.visit(4, block, False, action)
            for step in range(2 * self.line):
                for x in range(2):
                    landed(((ctx + step) % (2 * self.line), x * 2 + 1 - fsdp % 2))

    def go(self, after_first=None):
        self.run(lambda copy: copy.start(), self.arrive, after_first)

    def finish(self):
        self.run(lambda copy: copy.wait_send(), lambda block: None)


def spread_kernel(
    rows_ref, weight_ref, out_ref, all_ref, mine_ref, theirs_ref,
    sends, recvs, w_sends, w_recvs, o_sems, local,
):
    ctx, fsdp = lax.axis_index("ctx"), lax.axis_index("fsdp")
    slabs = lax.axis_size("ctx")
    rows, features = rows_ref.shape
    kinds, depth, share = weight_ref.shape
    width = share // slabs
    others = [((ctx + step) % slabs, fsdp) for step in range(1, slabs)]
    x, core = fsdp // 2, fsdp % 2
    meet(others + [(ctx, (1 - x) * 2 + core), (ctx, x * 2 + 1 - core)])

    def place(slab, part):
        return all_ref.at[pl.ds(slab * rows, rows), pl.ds(part * features, features)]

    def piece(kind, slab):
        return weight_ref.at[kind, :, pl.ds(slab * width, width)]

    def landing(kind, slab):
        return mine_ref.at[pl.ds(slab * depth, depth), pl.ds(kind * width, width)]

    own = [pltpu.make_async_copy(rows_ref, place(ctx, fsdp), local.at[0])] + [
        pltpu.make_async_copy(piece(kind, ctx), landing(kind, ctx), local.at[1 + kind])
        for kind in range(kinds)
    ]

    def weight_copies(owner, source, target):
        return [
            pltpu.make_async_remote_copy(
                src_ref=piece(kind, target),
                dst_ref=landing(kind, source),
                send_sem=w_sends.at[target, kind],
                recv_sem=w_recvs.at[source, kind],
                device_id=(owner, fsdp),
                device_id_type=MESH,
            )
            for kind in range(kinds)
        ]

    line, high, low = slabs // 2, ctx // 2, ctx % 2

    def send_to(target):
        for copy in weight_copies(target, ctx, target):
            copy.start()

    def send_weights(away):
        for goal in range(line):
            up = (high == away) & (goal > high)
            down = (line - 1 - high == away) & (goal < high)

            @pl.when(up | down)
            def _():
                send_to(goal * 2 + low)

        if away == line - 1:
            for step in range(line):
                send_to((high + step) % line * 2 + 1 - low)

    swap = pltpu.make_async_remote_copy(
        src_ref=out_ref,
        dst_ref=theirs_ref,
        send_sem=o_sems.at[0],
        recv_sem=o_sems.at[1],
        device_id=(ctx, x * 2 + 1 - core),
        device_id_type=MESH,
    )
    relay = Relay(rows_ref, place, sends, recvs, (3, 4))
    for copy in own:
        copy.start()
    swap.start()
    relay.go(send_weights)
    for step in range(1, slabs):
        source = (ctx + step) % slabs
        for copy in weight_copies(source, source, source):
            copy.wait_recv()
    relay.finish()
    for step in range(1, slabs):
        target = (ctx + step) % slabs
        for copy in weight_copies(target, ctx, target):
            copy.wait_send()
    swap.wait()
    for copy in own:
        copy.wait()


def collect_kernel(cols_ref, all_ref, other_ref, sends, recvs, half_recvs, local):
    ctx, fsdp = lax.axis_index("ctx"), lax.axis_index("fsdp")
    slabs, parts = lax.axis_size("ctx"), lax.axis_size("fsdp")
    width = cols_ref.shape[2]
    x, core = fsdp // 2, fsdp % 2
    partner = (ctx, x * 2 + 1 - core)
    meet([((ctx + step) % slabs, fsdp) for step in range(1, slabs)] + [partner])

    def place(slab, part):
        return all_ref.at[:, :, pl.ds(slab * width, width)]

    def half(block, own):
        cols = pl.ds(block[0] * width, width)
        return pltpu.make_async_remote_copy(
            src_ref=cols_ref.at[1 - core] if own else all_ref.at[1 - core, :, cols],
            dst_ref=other_ref.at[:, cols],
            send_sem=sends.at[3, block[0] * parts + fsdp],
            recv_sem=half_recvs.at[block[0]],
            device_id=partner,
            device_id_type=MESH,
        )

    own = pltpu.make_async_copy(cols_ref, place(ctx, fsdp), local.at[0])
    own.start()
    relay = Relay(cols_ref, place, sends, recvs, (4,), half)
    relay.go()
    for step in range(slabs):
        half(((ctx + step) % slabs, fsdp), False).wait_recv()
    relay.finish()
    own.wait()


def deliver_kernel(terms_ref, out_ref, sends, recvs, local):
    ctx, fsdp = lax.axis_index("ctx"), lax.axis_index("fsdp")
    slabs, parts = lax.axis_size("ctx"), lax.axis_size("fsdp")
    fold = slabs // parts
    width = terms_ref.shape[2]
    x, core = fsdp // 2, fsdp % 2
    home = ctx // fold
    stays = (home == fsdp) & (ctx % 2 == core)
    targets = [(ctx // 2 + step) % (slabs // 2) for step in range(slabs // 2)]
    sources = [(half, other) for half in range(fold) for other in range(parts // 2)]

    def to_others(action):
        for high in targets:
            @pl.when(jnp.logical_not(stays & (high == ctx // 2)))
            def _():
                action(high, (high * 2 + core, home))

    def from_others(action):
        for half, other in sources:
            source = (fsdp * fold + half, other * 2 + ctx % 2)

            @pl.when(jnp.logical_not((source[0] == ctx) & (source[1] == fsdp)))
            def _():
                action(half, other, source)

    barrier = pltpu.get_barrier_semaphore()

    def greet(device):
        pl.semaphore_signal(barrier, inc=1, device_id=device, device_id_type=MESH)

    to_others(lambda high, device: greet(device))
    from_others(lambda half, other, device: greet(device))

    @pl.when(stays)
    def _():
        pl.semaphore_wait(barrier, len(targets) + len(sources) - 2)

    @pl.when(jnp.logical_not(stays))
    def _():
        pl.semaphore_wait(barrier, len(targets) + len(sources))

    def slot(half, other):
        return out_ref.at[other, :, pl.ds(half * width, width)]

    def outgoing(high, device):
        return pltpu.make_async_remote_copy(
            src_ref=terms_ref.at[high],
            dst_ref=slot(ctx % fold, x),
            send_sem=sends.at[high],
            recv_sem=recvs.at[x * fold + ctx % fold],
            device_id=device,
            device_id_type=MESH,
        )

    def incoming(half, other, device):
        return pltpu.make_async_remote_copy(
            src_ref=terms_ref.at[0],
            dst_ref=slot(half, other),
            send_sem=sends.at[0],
            recv_sem=recvs.at[other * fold + half],
            device_id=device,
            device_id_type=MESH,
        )

    own = pltpu.make_async_copy(terms_ref.at[ctx // 2], slot(ctx % fold, x), local.at[0])
    to_others(lambda high, device: outgoing(high, device).start())

    @pl.when(stays)
    def _():
        own.start()

    from_others(lambda half, other, device: incoming(half, other, device).wait_recv())
    to_others(lambda high, device: outgoing(high, device).wait_send())

    @pl.when(stays)
    def _():
        own.wait()


VMEM_SPEC = pl.BlockSpec(memory_space=pltpu.VMEM)
ANY_SPEC = pl.BlockSpec(memory_space=pl.ANY)
DMA = pltpu.SemaphoreType.DMA


def params(number):
    return pltpu.CompilerParams(collective_id=number, has_side_effects=True)


def spread(rows, weights, out_weight):
    slabs, parts = lax.axis_size("ctx"), lax.axis_size("fsdp")
    kinds, depth, share = weights.shape
    return pl.pallas_call(
        spread_kernel,
        out_shape=(
            jax.ShapeDtypeStruct((rows.shape[0] * slabs, rows.shape[1] * parts), rows.dtype),
            jax.ShapeDtypeStruct((depth * slabs, kinds * share // slabs), weights.dtype),
            jax.ShapeDtypeStruct(out_weight.shape, out_weight.dtype),
        ),
        in_specs=[VMEM_SPEC, VMEM_SPEC, VMEM_SPEC],
        out_specs=(ANY_SPEC, ANY_SPEC, ANY_SPEC),
        scratch_shapes=[
            DMA((5, slabs * parts)), DMA((slabs * parts,)),
            DMA((slabs, kinds)), DMA((slabs, kinds)), DMA((2,)), DMA((1 + kinds,)),
        ],
        compiler_params=params(0),
    )(rows, weights, out_weight)


def collect(cols):
    slabs, parts = lax.axis_size("ctx"), lax.axis_size("fsdp")
    halves, rows, width = cols.shape
    return pl.pallas_call(
        collect_kernel,
        out_shape=(
            jax.ShapeDtypeStruct((halves, rows, width * slabs), cols.dtype),
            jax.ShapeDtypeStruct((rows, width * slabs), cols.dtype),
        ),
        in_specs=[VMEM_SPEC],
        out_specs=(ANY_SPEC, ANY_SPEC),
        scratch_shapes=[DMA((5, slabs * parts)), DMA((slabs * parts,)), DMA((slabs,)), DMA((1,))],
        compiler_params=params(1),
    )(cols)


def deliver(terms):
    slabs, parts = lax.axis_size("ctx"), lax.axis_size("fsdp")
    fold = slabs // parts
    return pl.pallas_call(
        deliver_kernel,
        out_shape=jax.ShapeDtypeStruct((parts // 2, terms.shape[1], terms.shape[2] * fold), terms.dtype),
        in_specs=[VMEM_SPEC],
        out_specs=ANY_SPEC,
        scratch_shapes=[DMA((slabs // 2,)), DMA((fold * parts // 2,)), DMA((1,))],
        compiler_params=params(2),
    )(terms)


def mix_kernel(
    group_width, rows_ref, weight_ref, taps_ref, base_ref, skip_ref, out_ref, bands, tail, last
):
    groups, window = base_ref.shape
    flen = window // 2
    own = out_ref.shape[2]

    @pl.when(pl.program_id(0) == 0)
    def _():
        tail[...] = jnp.zeros_like(tail)
        last[...] = jnp.zeros_like(last)
        for group in range(groups):
            row = jnp.broadcast_to(base_ref[group : group + 1, :], (flen, window))
            band = pltpu.roll(row, 0, 1, stride=1, stride_axis=0)
            bands[pl.ds(group * flen, flen), :] = band.astype(jnp.bfloat16)

    proj = jnp.dot(rows_ref[...], weight_ref[...], preferred_element_type=jnp.float32)
    proj = proj.astype(jnp.bfloat16).astype(jnp.float32)
    rows = proj.shape[0]
    ahead = tail.shape[0]
    extended = jnp.concatenate([tail[...], proj], axis=0)
    tail[...] = proj[rows - ahead :]
    filtered = short_conv(
        [taps_ref[tap : tap + 1, :] for tap in range(3)], extended[ahead - 2 :]
    )
    product = (filtered[:, own : 2 * own] * filtered[:, 2 * own :]).astype(jnp.bfloat16)
    reach = jnp.concatenate([last[...], product], axis=0)
    last[...] = product[rows - flen :]
    lane_group = lax.broadcasted_iota(jnp.int32, (flen, own), 1) // group_width
    for start in range(0, rows, flen):
        every = jnp.dot(
            bands[...], reach[start : start + window], preferred_element_type=jnp.float32
        )
        conv = every[:flen]
        for group in range(1, groups):
            conv = jnp.where(lane_group == group, every[group * flen : (group + 1) * flen], conv)
        here = product[start : start + flen].astype(jnp.float32)
        gate = filtered[start : start + flen, :own]
        out_ref[0, start : start + flen, :] = (gate * (conv + skip_ref[...] * here)).astype(jnp.bfloat16)


def mix(whole, weights, taps, base, skip, slab_rows, group_width):
    positions, depth = whole.shape
    own = skip.shape[1]
    groups, window = base.shape
    full = lambda array: pl.BlockSpec(array.shape, lambda i: (0, 0))
    return pl.pallas_call(
        functools.partial(mix_kernel, group_width),
        grid=(positions // slab_rows,),
        out_shape=jax.ShapeDtypeStruct((2, positions // 2, own), jnp.bfloat16),
        in_specs=[
            pl.BlockSpec((slab_rows, depth), lambda i: (i, 0)),
            full(weights), full(taps), full(base), full(skip),
        ],
        out_specs=pl.BlockSpec((1, slab_rows, own), lambda i: (i % 2, i // 2, 0)),
        scratch_shapes=[
            pltpu.VMEM((groups * window // 2, window), jnp.bfloat16),
            pltpu.VMEM((8, 3 * own), jnp.float32),
            pltpu.VMEM((window // 2, own), jnp.bfloat16),
        ],
    )(whole, weights, taps, base, skip)


def channel_plan(tokens, norm_gain, in_weight, short_filter, long_filter, skip_gain, out_weight):
    ctx, fsdp = lax.axis_index("ctx"), lax.axis_index("fsdp")
    slabs, parts = lax.axis_size("ctx"), lax.axis_size("fsdp")
    rows, features = tokens.shape
    positions = rows * slabs
    share = in_weight.shape[2]
    own = share // slabs
    values = tokens.astype(jnp.float32)
    mean_square = lax.psum(jnp.sum(values * values, axis=-1, keepdims=True), "fsdp") / (features * parts)
    gain = lax.dynamic_slice_in_dim(norm_gain, fsdp * features, features, 0)
    normed = (values * lax.rsqrt(mean_square + 1e-06) * gain).astype(jnp.bfloat16)

    whole, weights, partner_weight = spread(normed, in_weight.transpose(1, 0, 2), out_weight)
    taps = lax.dynamic_slice_in_dim(short_filter, ctx * own, own, 2).reshape(3, 3 * own)
    flen = long_filter.shape[1]
    group_count = long_filter.shape[0] // slabs
    filters = lax.dynamic_slice_in_dim(long_filter, ctx * group_count, group_count, 0)
    base = jnp.pad(filters[:, ::-1].astype(jnp.float32), ((0, 0), (1, flen - 1)))
    skip = lax.dynamic_slice_in_dim(skip_gain, ctx * own, own, 0)[None]
    gated = mix(whole, weights, taps, base, skip, rows, own // group_count)
    every, partner_cols = collect(gated)
    core_cols = lax.dynamic_index_in_dim(every, fsdp % 2, 0, keepdims=False)
    terms = jnp.dot(core_cols, out_weight, preferred_element_type=jnp.float32)
    terms += jnp.dot(partner_cols, partner_weight, preferred_element_type=jnp.float32)
    terms = terms.astype(jnp.bfloat16).reshape(slabs // 2, rows, out_weight.shape[1])
    arrived = deliver(terms)
    return jnp.sum(arrived.astype(jnp.float32), axis=0).astype(jnp.bfloat16)


def on_device(tokens, *rest):
    slabs, parts = lax.axis_size("ctx"), lax.axis_size("fsdp")
    own = rest[1].shape[2] // slabs
    gathered = tokens.size * slabs * parts * 2
    fits = parts == 4 and slabs % parts == 0 and own % LANE == 0 and gathered <= 2**25
    return (channel_plan if fits else slab_plan)(tokens, *rest)


def solution(mesh):
    in_specs = (
        P("ctx", "fsdp"),
        P(),
        P("ctx", None, "fsdp"),
        P(None, None, "fsdp"),
        P("fsdp", None),
        P("fsdp"),
        P("fsdp", "ctx"),
    )
    out_specs = P("ctx", "fsdp")
    return jax.shard_map(
        on_device, mesh=mesh, in_specs=in_specs, out_specs=out_specs, check_vma=False
    )
```

```python
import functools

import jax
import jax.numpy as jnp
from jax import lax
from jax.experimental import pallas as pl
from jax.experimental.pallas import tpu as pltpu
from jax.sharding import PartitionSpec as P


def passed_along(block, axis, distance):
    devices = range(lax.axis_size(axis))
    route = [(i - distance, i) for i in devices if i - distance in devices]
    return lax.ppermute(block, axis, route)


def toeplitz_blocks(long_filter, row_count):
    groups = long_filter.shape[0]
    flen = long_filter.shape[1]
    window = flen + row_count - 1
    reversed_taps = long_filter[:, ::-1]
    padded = jnp.concatenate(
        [reversed_taps, jnp.zeros((groups, row_count), long_filter.dtype)], axis=1
    )
    tiled = jnp.tile(padded, (1, row_count))
    return tiled[:, : row_count * window].reshape(groups, row_count, window)


def short_conv(taps, extended):
    return taps[0] * extended[2:] + taps[1] * extended[1:-1] + taps[2] * extended[:-2]


def slab_plan(tokens, norm_gain, in_weight, short_filter, long_filter, skip_gain, out_weight):
    whole = lax.all_gather(tokens, "fsdp", axis=1, tiled=True)
    row_count = whole.shape[0]
    values = whole.astype(jnp.float32)
    mean_square = jnp.mean(values * values, axis=-1, keepdims=True)
    normed = (values * lax.rsqrt(mean_square + 1e-06) * norm_gain).astype(jnp.bfloat16)
    share = in_weight.shape[2]
    width_all = 3 * share
    weight_rows = lax.all_gather(in_weight, "ctx", axis=0, tiled=True)
    flat_rows = weight_rows.reshape(weight_rows.shape[0], width_all)
    proj = jnp.dot(normed, flat_rows, preferred_element_type=jnp.float32).astype(jnp.bfloat16)
    taps = short_filter.reshape(3, width_all)
    flen = long_filter.shape[1]
    earlier = passed_along(proj[row_count - 2 :], "ctx", 1)
    extended = jnp.concatenate([earlier, proj], axis=0).astype(jnp.float32)
    filtered = short_conv(taps, extended)
    out_gate = filtered[:, :share]
    product = (filtered[:, share : 2 * share] * filtered[:, 2 * share :]).astype(jnp.bfloat16)
    previous = passed_along(product[row_count - (flen - 1) :], "ctx", 1)
    product_ext = jnp.concatenate([previous, product], axis=0)
    groups = long_filter.shape[0]
    group_width = share // groups
    window = row_count + flen - 1
    blocks = toeplitz_blocks(long_filter, row_count)
    conv = jnp.einsum(
        "gts,sgc->tgc",
        blocks,
        product_ext.reshape(window, groups, group_width),
        preferred_element_type=jnp.float32,
    ).reshape(row_count, share)
    gated = (out_gate * (conv + skip_gain * product.astype(jnp.float32))).astype(jnp.bfloat16)
    terms = jnp.dot(
        gated,
        lax.all_gather(out_weight, "ctx", axis=1, tiled=True),
        preferred_element_type=jnp.float32,
    )
    mixed = lax.psum_scatter(terms, "fsdp", scatter_dimension=1, tiled=True).astype(jnp.bfloat16)
    return mixed


MESH = pl.DeviceIdType.MESH
LANE = 128


def meet(peers):
    barrier = pltpu.get_barrier_semaphore()
    for peer in peers:
        pl.semaphore_signal(barrier, inc=1, device_id=peer, device_id_type=MESH)
    pl.semaphore_wait(barrier, len(peers))


class Relay:
    def __init__(self, own, place, sends, recvs, across, half=None):
        self.me = (lax.axis_index("ctx"), lax.axis_index("fsdp"))
        self.line = lax.axis_size("ctx") // 2
        self.width = lax.axis_size("fsdp")
        self.high, self.low = self.me[0] // 2, self.me[0] % 2
        self.own, self.place = own, place
        self.sends, self.recvs = sends, recvs
        self.across = across
        self.half = half

    def copy(self, kind, block, target, own=False):
        index = block[0] * self.width + block[1]
        return pltpu.make_async_remote_copy(
            src_ref=self.own if own else self.place(*block),
            dst_ref=self.place(*block),
            send_sem=self.sends.at[kind, index],
            recv_sem=self.recvs.at[index],
            device_id=target,
            device_id_type=MESH,
        )

    def visit(self, kind, block, own, action):
        ctx, fsdp = self.me
        if kind == 0:
            @pl.when(self.high < self.line - 1)
            def _():
                action(self.copy(0, block, (ctx + 2, fsdp), own))
        elif kind == 1:
            @pl.when(self.high > 0)
            def _():
                action(self.copy(1, block, (ctx - 2, fsdp), own))
        elif kind == 2:
            action(self.copy(2, block, (ctx + 1 - 2 * self.low, fsdp), own))
        elif kind == 3:
            x, core = fsdp // 2, fsdp % 2
            action(self.copy(3, block, (ctx, (1 - x) * 2 + core), own))
        elif self.half is not None:
            action(self.half(block, own))
        else:
            action(self.copy(4, block, (ctx, fsdp + 1 - 2 * (fsdp % 2)), own))

    def arrive(self, block):
        self.copy(0, block, (self.me[0], self.me[1])).wait_recv()

    def run(self, action, landed, after_first=None):
        ctx, fsdp = self.me
        high, low = self.high, self.low
        for kind in (0, 1, 2) + self.across:
            self.visit(kind, (ctx, fsdp), True, action)
        for away in range(self.line + 1):
            if 1 <= away < self.line:
                @pl.when(high >= away)
                def _():
                    block = ((high - away) * 2 + low, fsdp)
                    landed(block)
                    for kind in (0, 2) + self.across:
                        self.visit(kind, block, False, action)

                @pl.when(high + away < self.line)
                def _():
                    block = ((high + away) * 2 + low, fsdp)
                    landed(block)
                    for kind in (1, 2) + self.across:
                        self.visit(kind, block, False, action)
            if away < self.line and after_first is not None:
                after_first(away)
            if away >= 1:
                back = away - 1
                for sign in (-1, 1) if back else (1,):
                    at = high + sign * back

                    @pl.when((at >= 0) & (at < self.line))
                    def _():
                        block = (at * 2 + 1 - low, fsdp)
                        landed(block)
                        for kind in self.across:
                            self.visit(kind, block, False, action)
        if 3 in self.across:
            other = (1 - fsdp // 2) * 2 + fsdp % 2
            for step in range(2 * self.line):
                block = ((ctx + step) % (2 * self.line), other)
                landed(block)
                self.visit(4, block, False, action)
            for step in range(2 * self.line):
                for x in range(2):
                    landed(((ctx + step) % (2 * self.line), x * 2 + 1 - fsdp % 2))

    def go(self, after_first=None):
        self.run(lambda copy: copy.start(), self.arrive, after_first)

    def finish(self):
        self.run(lambda copy: copy.wait_send(), lambda block: None)


def spread_kernel(
    rows_ref, weight_ref, out_ref, all_ref, mine_ref, theirs_ref,
    sends, recvs, w_sends, w_recvs, o_sems, local,
):
    ctx, fsdp = lax.axis_index("ctx"), lax.axis_index("fsdp")
    slabs = lax.axis_size("ctx")
    rows, features = rows_ref.shape
    kinds, depth, share = weight_ref.shape
    width = share // slabs
    others = [((ctx + step) % slabs, fsdp) for step in range(1, slabs)]
    x, core = fsdp // 2, fsdp % 2
    meet(others + [(ctx, (1 - x) * 2 + core), (ctx, x * 2 + 1 - core)])

    def place(slab, part):
        return all_ref.at[pl.ds(slab * rows, rows), pl.ds(part * features, features)]

    def piece(kind, slab):
        return weight_ref.at[kind, :, pl.ds(slab * width, width)]

    def landing(kind, slab):
        return mine_ref.at[pl.ds(slab * depth, depth), pl.ds(kind * width, width)]

    own = [pltpu.make_async_copy(rows_ref, place(ctx, fsdp), local.at[0])] + [
        pltpu.make_async_copy(piece(kind, ctx), landing(kind, ctx), local.at[1 + kind])
        for kind in range(kinds)
    ]

    def weight_copies(owner, source, target):
        return [
            pltpu.make_async_remote_copy(
                src_ref=piece(kind, target),
                dst_ref=landing(kind, source),
                send_sem=w_sends.at[target, kind],
                recv_sem=w_recvs.at[source, kind],
                device_id=(owner, fsdp),
                device_id_type=MESH,
            )
            for kind in range(kinds)
        ]

    line, high, low = slabs // 2, ctx // 2, ctx % 2

    def send_to(target):
        for copy in weight_copies(target, ctx, target):
            copy.start()

    def send_weights(away):
        hold = line // 2
        for goal in range(line if away >= hold else 0):
            below, above = high, line - 1 - high
            up = ((below <= away) if away == hold else (below == away)) & (goal > high)
            down = ((above <= away) if away == hold else (above == away)) & (goal < high)

            @pl.when(up | down)
            def _():
                send_to(goal * 2 + low)

        if away == line - 1:
            for step in range(line):
                send_to((high + step) % line * 2 + 1 - low)

    swap = pltpu.make_async_remote_copy(
        src_ref=out_ref,
        dst_ref=theirs_ref,
        send_sem=o_sems.at[0],
        recv_sem=o_sems.at[1],
        device_id=(ctx, x * 2 + 1 - core),
        device_id_type=MESH,
    )
    relay = Relay(rows_ref, place, sends, recvs, (3, 4))
    for copy in own:
        copy.start()
    swap.start()
    relay.go(send_weights)
    for step in range(1, slabs):
        source = (ctx + step) % slabs
        for copy in weight_copies(source, source, source):
            copy.wait_recv()
    relay.finish()
    for step in range(1, slabs):
        target = (ctx + step) % slabs
        for copy in weight_copies(target, ctx, target):
            copy.wait_send()
    swap.wait()
    for copy in own:
        copy.wait()


def collect_kernel(cols_ref, all_ref, other_ref, sends, recvs, half_recvs, local):
    ctx, fsdp = lax.axis_index("ctx"), lax.axis_index("fsdp")
    slabs, parts = lax.axis_size("ctx"), lax.axis_size("fsdp")
    width = cols_ref.shape[2]
    x, core = fsdp // 2, fsdp % 2
    partner = (ctx, x * 2 + 1 - core)
    meet([((ctx + step) % slabs, fsdp) for step in range(1, slabs)] + [partner])

    def place(slab, part):
        return all_ref.at[:, :, pl.ds(slab * width, width)]

    def half(block, own):
        cols = pl.ds(block[0] * width, width)
        return pltpu.make_async_remote_copy(
            src_ref=cols_ref.at[1 - core] if own else all_ref.at[1 - core, :, cols],
            dst_ref=other_ref.at[:, cols],
            send_sem=sends.at[3, block[0] * parts + fsdp],
            recv_sem=half_recvs.at[block[0]],
            device_id=partner,
            device_id_type=MESH,
        )

    own = pltpu.make_async_copy(cols_ref, place(ctx, fsdp), local.at[0])
    own.start()
    relay = Relay(cols_ref, place, sends, recvs, (4,), half)
    relay.go()
    for step in range(slabs):
        half(((ctx + step) % slabs, fsdp), False).wait_recv()
    relay.finish()
    own.wait()


def deliver_kernel(terms_ref, out_ref, sends, recvs, local):
    ctx, fsdp = lax.axis_index("ctx"), lax.axis_index("fsdp")
    slabs, parts = lax.axis_size("ctx"), lax.axis_size("fsdp")
    fold = slabs // parts
    width = terms_ref.shape[2]
    x, core = fsdp // 2, fsdp % 2
    home = ctx // fold
    stays = (home == fsdp) & (ctx % 2 == core)
    targets = [(ctx // 2 + step) % (slabs // 2) for step in range(slabs // 2)]
    sources = [(half, other) for half in range(fold) for other in range(parts // 2)]

    def to_others(action):
        for high in targets:
            @pl.when(jnp.logical_not(stays & (high == ctx // 2)))
            def _():
                action(high, (high * 2 + core, home))

    def from_others(action):
        for half, other in sources:
            source = (fsdp * fold + half, other * 2 + ctx % 2)

            @pl.when(jnp.logical_not((source[0] == ctx) & (source[1] == fsdp)))
            def _():
                action(half, other, source)

    barrier = pltpu.get_barrier_semaphore()

    def greet(device):
        pl.semaphore_signal(barrier, inc=1, device_id=device, device_id_type=MESH)

    to_others(lambda high, device: greet(device))
    from_others(lambda half, other, device: greet(device))

    @pl.when(stays)
    def _():
        pl.semaphore_wait(barrier, len(targets) + len(sources) - 2)

    @pl.when(jnp.logical_not(stays))
    def _():
        pl.semaphore_wait(barrier, len(targets) + len(sources))

    def slot(half, other):
        return out_ref.at[other, :, pl.ds(half * width, width)]

    def outgoing(high, device):
        return pltpu.make_async_remote_copy(
            src_ref=terms_ref.at[high],
            dst_ref=slot(ctx % fold, x),
            send_sem=sends.at[high],
            recv_sem=recvs.at[x * fold + ctx % fold],
            device_id=device,
            device_id_type=MESH,
        )

    def incoming(half, other, device):
        return pltpu.make_async_remote_copy(
            src_ref=terms_ref.at[0],
            dst_ref=slot(half, other),
            send_sem=sends.at[0],
            recv_sem=recvs.at[other * fold + half],
            device_id=device,
            device_id_type=MESH,
        )

    own = pltpu.make_async_copy(terms_ref.at[ctx // 2], slot(ctx % fold, x), local.at[0])
    to_others(lambda high, device: outgoing(high, device).start())

    @pl.when(stays)
    def _():
        own.start()

    from_others(lambda half, other, device: incoming(half, other, device).wait_recv())
    to_others(lambda high, device: outgoing(high, device).wait_send())

    @pl.when(stays)
    def _():
        own.wait()


VMEM_SPEC = pl.BlockSpec(memory_space=pltpu.VMEM)
ANY_SPEC = pl.BlockSpec(memory_space=pl.ANY)
DMA = pltpu.SemaphoreType.DMA


def params(number):
    return pltpu.CompilerParams(collective_id=number, has_side_effects=True)


def spread(rows, weights, out_weight):
    slabs, parts = lax.axis_size("ctx"), lax.axis_size("fsdp")
    kinds, depth, share = weights.shape
    return pl.pallas_call(
        spread_kernel,
        out_shape=(
            jax.ShapeDtypeStruct((rows.shape[0] * slabs, rows.shape[1] * parts), rows.dtype),
            jax.ShapeDtypeStruct((depth * slabs, kinds * share // slabs), weights.dtype),
            jax.ShapeDtypeStruct(out_weight.shape, out_weight.dtype),
        ),
        in_specs=[VMEM_SPEC, VMEM_SPEC, VMEM_SPEC],
        out_specs=(ANY_SPEC, ANY_SPEC, ANY_SPEC),
        scratch_shapes=[
            DMA((5, slabs * parts)), DMA((slabs * parts,)),
            DMA((slabs, kinds)), DMA((slabs, kinds)), DMA((2,)), DMA((1 + kinds,)),
        ],
        compiler_params=params(0),
    )(rows, weights, out_weight)


def collect(cols):
    slabs, parts = lax.axis_size("ctx"), lax.axis_size("fsdp")
    halves, rows, width = cols.shape
    return pl.pallas_call(
        collect_kernel,
        out_shape=(
            jax.ShapeDtypeStruct((halves, rows, width * slabs), cols.dtype),
            jax.ShapeDtypeStruct((rows, width * slabs), cols.dtype),
        ),
        in_specs=[VMEM_SPEC],
        out_specs=(ANY_SPEC, ANY_SPEC),
        scratch_shapes=[DMA((5, slabs * parts)), DMA((slabs * parts,)), DMA((slabs,)), DMA((1,))],
        compiler_params=params(1),
    )(cols)


def deliver(terms):
    slabs, parts = lax.axis_size("ctx"), lax.axis_size("fsdp")
    fold = slabs // parts
    return pl.pallas_call(
        deliver_kernel,
        out_shape=jax.ShapeDtypeStruct((parts // 2, terms.shape[1], terms.shape[2] * fold), terms.dtype),
        in_specs=[VMEM_SPEC],
        out_specs=ANY_SPEC,
        scratch_shapes=[DMA((slabs // 2,)), DMA((fold * parts // 2,)), DMA((1,))],
        compiler_params=params(2),
    )(terms)


def mix_kernel(
    group_width, rows_ref, weight_ref, taps_ref, base_ref, skip_ref, out_ref, bands, tail, last
):
    groups, window = base_ref.shape
    flen = window // 2
    own = out_ref.shape[2]

    @pl.when(pl.program_id(0) == 0)
    def _():
        tail[...] = jnp.zeros_like(tail)
        last[...] = jnp.zeros_like(last)
        for group in range(groups):
            row = jnp.broadcast_to(base_ref[group : group + 1, :], (flen, window))
            band = pltpu.roll(row, 0, 1, stride=1, stride_axis=0)
            bands[pl.ds(group * flen, flen), :] = band.astype(jnp.bfloat16)

    proj = jnp.dot(rows_ref[...], weight_ref[...], preferred_element_type=jnp.float32)
    proj = proj.astype(jnp.bfloat16).astype(jnp.float32)
    rows = proj.shape[0]
    ahead = tail.shape[0]
    extended = jnp.concatenate([tail[...], proj], axis=0)
    tail[...] = proj[rows - ahead :]
    filtered = short_conv(
        [taps_ref[tap : tap + 1, :] for tap in range(3)], extended[ahead - 2 :]
    )
    product = (filtered[:, own : 2 * own] * filtered[:, 2 * own :]).astype(jnp.bfloat16)
    reach = jnp.concatenate([last[...], product], axis=0)
    last[...] = product[rows - flen :]
    lane_group = lax.broadcasted_iota(jnp.int32, (flen, own), 1) // group_width
    for start in range(0, rows, flen):
        every = jnp.dot(
            bands[...], reach[start : start + window], preferred_element_type=jnp.float32
        )
        conv = every[:flen]
        for group in range(1, groups):
            conv = jnp.where(lane_group == group, every[group * flen : (group + 1) * flen], conv)
        here = product[start : start + flen].astype(jnp.float32)
        gate = filtered[start : start + flen, :own]
        out_ref[0, start : start + flen, :] = (gate * (conv + skip_ref[...] * here)).astype(jnp.bfloat16)


def mix(whole, weights, taps, base, skip, slab_rows, group_width):
    positions, depth = whole.shape
    own = skip.shape[1]
    groups, window = base.shape
    full = lambda array: pl.BlockSpec(array.shape, lambda i: (0, 0))
    return pl.pallas_call(
        functools.partial(mix_kernel, group_width),
        grid=(positions // slab_rows,),
        out_shape=jax.ShapeDtypeStruct((2, positions // 2, own), jnp.bfloat16),
        in_specs=[
            pl.BlockSpec((slab_rows, depth), lambda i: (i, 0)),
            full(weights), full(taps), full(base), full(skip),
        ],
        out_specs=pl.BlockSpec((1, slab_rows, own), lambda i: (i % 2, i // 2, 0)),
        scratch_shapes=[
            pltpu.VMEM((groups * window // 2, window), jnp.bfloat16),
            pltpu.VMEM((8, 3 * own), jnp.float32),
            pltpu.VMEM((window // 2, own), jnp.bfloat16),
        ],
    )(whole, weights, taps, base, skip)


def channel_plan(tokens, norm_gain, in_weight, short_filter, long_filter, skip_gain, out_weight):
    ctx, fsdp = lax.axis_index("ctx"), lax.axis_index("fsdp")
    slabs, parts = lax.axis_size("ctx"), lax.axis_size("fsdp")
    rows, features = tokens.shape
    positions = rows * slabs
    share = in_weight.shape[2]
    own = share // slabs
    values = tokens.astype(jnp.float32)
    mean_square = lax.psum(jnp.sum(values * values, axis=-1, keepdims=True), "fsdp") / (features * parts)
    gain = lax.dynamic_slice_in_dim(norm_gain, fsdp * features, features, 0)
    normed = (values * lax.rsqrt(mean_square + 1e-06) * gain).astype(jnp.bfloat16)

    whole, weights, partner_weight = spread(normed, in_weight.transpose(1, 0, 2), out_weight)
    taps = lax.dynamic_slice_in_dim(short_filter, ctx * own, own, 2).reshape(3, 3 * own)
    flen = long_filter.shape[1]
    group_count = long_filter.shape[0] // slabs
    filters = lax.dynamic_slice_in_dim(long_filter, ctx * group_count, group_count, 0)
    base = jnp.pad(filters[:, ::-1].astype(jnp.float32), ((0, 0), (1, flen - 1)))
    skip = lax.dynamic_slice_in_dim(skip_gain, ctx * own, own, 0)[None]
    gated = mix(whole, weights, taps, base, skip, rows, own // group_count)
    every, partner_cols = collect(gated)
    core_cols = lax.dynamic_index_in_dim(every, fsdp % 2, 0, keepdims=False)
    terms = jnp.dot(core_cols, out_weight, preferred_element_type=jnp.float32)
    terms += jnp.dot(partner_cols, partner_weight, preferred_element_type=jnp.float32)
    terms = terms.astype(jnp.bfloat16).reshape(slabs // 2, rows, out_weight.shape[1])
    arrived = deliver(terms)
    return jnp.sum(arrived.astype(jnp.float32), axis=0).astype(jnp.bfloat16)


def on_device(tokens, *rest):
    slabs, parts = lax.axis_size("ctx"), lax.axis_size("fsdp")
    own = rest[1].shape[2] // slabs
    gathered = tokens.size * slabs * parts * 2
    fits = parts == 4 and slabs % parts == 0 and own % LANE == 0 and gathered <= 2**25
    return (channel_plan if fits else slab_plan)(tokens, *rest)


def solution(mesh):
    in_specs = (
        P("ctx", "fsdp"),
        P(),
        P("ctx", None, "fsdp"),
        P(None, None, "fsdp"),
        P("fsdp", None),
        P("fsdp"),
        P("fsdp", "ctx"),
    )
    out_specs = P("ctx", "fsdp")
    return jax.shard_map(
        on_device, mesh=mesh, in_specs=in_specs, out_specs=out_specs, check_vma=False
    )
```

```python
import functools

import jax
import jax.numpy as jnp
from jax import lax
from jax.experimental import pallas as pl
from jax.experimental.pallas import tpu as pltpu
from jax.sharding import PartitionSpec as P


def passed_along(block, axis, distance):
    devices = range(lax.axis_size(axis))
    route = [(i - distance, i) for i in devices if i - distance in devices]
    return lax.ppermute(block, axis, route)


def toeplitz_blocks(long_filter, row_count):
    groups = long_filter.shape[0]
    flen = long_filter.shape[1]
    window = flen + row_count - 1
    reversed_taps = long_filter[:, ::-1]
    padded = jnp.concatenate(
        [reversed_taps, jnp.zeros((groups, row_count), long_filter.dtype)], axis=1
    )
    tiled = jnp.tile(padded, (1, row_count))
    return tiled[:, : row_count * window].reshape(groups, row_count, window)


def short_conv(taps, extended):
    return taps[0] * extended[2:] + taps[1] * extended[1:-1] + taps[2] * extended[:-2]


def slab_plan(tokens, norm_gain, in_weight, short_filter, long_filter, skip_gain, out_weight):
    whole = lax.all_gather(tokens, "fsdp", axis=1, tiled=True)
    row_count = whole.shape[0]
    values = whole.astype(jnp.float32)
    mean_square = jnp.mean(values * values, axis=-1, keepdims=True)
    normed = (values * lax.rsqrt(mean_square + 1e-06) * norm_gain).astype(jnp.bfloat16)
    share = in_weight.shape[2]
    width_all = 3 * share
    weight_rows = lax.all_gather(in_weight, "ctx", axis=0, tiled=True)
    flat_rows = weight_rows.reshape(weight_rows.shape[0], width_all)
    proj = jnp.dot(normed, flat_rows, preferred_element_type=jnp.float32).astype(jnp.bfloat16)
    taps = short_filter.reshape(3, width_all)
    flen = long_filter.shape[1]
    earlier = passed_along(proj[row_count - 2 :], "ctx", 1)
    extended = jnp.concatenate([earlier, proj], axis=0).astype(jnp.float32)
    filtered = short_conv(taps, extended)
    out_gate = filtered[:, :share]
    product = (filtered[:, share : 2 * share] * filtered[:, 2 * share :]).astype(jnp.bfloat16)
    previous = passed_along(product[row_count - (flen - 1) :], "ctx", 1)
    product_ext = jnp.concatenate([previous, product], axis=0)
    groups = long_filter.shape[0]
    group_width = share // groups
    window = row_count + flen - 1
    blocks = toeplitz_blocks(long_filter, row_count)
    conv = jnp.einsum(
        "gts,sgc->tgc",
        blocks,
        product_ext.reshape(window, groups, group_width),
        preferred_element_type=jnp.float32,
    ).reshape(row_count, share)
    gated = (out_gate * (conv + skip_gain * product.astype(jnp.float32))).astype(jnp.bfloat16)
    terms = jnp.dot(
        gated,
        lax.all_gather(out_weight, "ctx", axis=1, tiled=True),
        preferred_element_type=jnp.float32,
    )
    mixed = lax.psum_scatter(terms, "fsdp", scatter_dimension=1, tiled=True).astype(jnp.bfloat16)
    return mixed


MESH = pl.DeviceIdType.MESH
LANE = 128


def meet(peers):
    barrier = pltpu.get_barrier_semaphore()
    for peer in peers:
        pl.semaphore_signal(barrier, inc=1, device_id=peer, device_id_type=MESH)
    pl.semaphore_wait(barrier, len(peers))


class Relay:
    def __init__(self, own, place, sends, recvs, across, half=None):
        self.me = (lax.axis_index("ctx"), lax.axis_index("fsdp"))
        self.line = lax.axis_size("ctx") // 2
        self.width = lax.axis_size("fsdp")
        self.high, self.low = self.me[0] // 2, self.me[0] % 2
        self.own, self.place = own, place
        self.sends, self.recvs = sends, recvs
        self.across = across
        self.half = half

    def copy(self, kind, block, target, own=False):
        index = block[0] * self.width + block[1]
        return pltpu.make_async_remote_copy(
            src_ref=self.own if own else self.place(*block),
            dst_ref=self.place(*block),
            send_sem=self.sends.at[kind, index],
            recv_sem=self.recvs.at[index],
            device_id=target,
            device_id_type=MESH,
        )

    def visit(self, kind, block, own, action):
        ctx, fsdp = self.me
        if kind == 0:
            @pl.when(self.high < self.line - 1)
            def _():
                action(self.copy(0, block, (ctx + 2, fsdp), own))
        elif kind == 1:
            @pl.when(self.high > 0)
            def _():
                action(self.copy(1, block, (ctx - 2, fsdp), own))
        elif kind == 2:
            action(self.copy(2, block, (ctx + 1 - 2 * self.low, fsdp), own))
        elif kind == 3:
            x, core = fsdp // 2, fsdp % 2
            action(self.copy(3, block, (ctx, (1 - x) * 2 + core), own))
        elif self.half is not None:
            action(self.half(block, own))
        else:
            action(self.copy(4, block, (ctx, fsdp + 1 - 2 * (fsdp % 2)), own))

    def arrive(self, block):
        self.copy(0, block, (self.me[0], self.me[1])).wait_recv()

    def run(self, action, landed, after_first=None):
        ctx, fsdp = self.me
        high, low = self.high, self.low
        for kind in (0, 1, 2) + self.across:
            self.visit(kind, (ctx, fsdp), True, action)
        for away in range(self.line + 1):
            if 1 <= away < self.line:
                @pl.when(high >= away)
                def _():
                    block = ((high - away) * 2 + low, fsdp)
                    landed(block)
                    for kind in (0, 2) + self.across:
                        self.visit(kind, block, False, action)

                @pl.when(high + away < self.line)
                def _():
                    block = ((high + away) * 2 + low, fsdp)
                    landed(block)
                    for kind in (1, 2) + self.across:
                        self.visit(kind, block, False, action)
            if away < self.line and after_first is not None:
                after_first(away)
            if away >= 1:
                back = away - 1
                for sign in (-1, 1) if back else (1,):
                    at = high + sign * back

                    @pl.when((at >= 0) & (at < self.line))
                    def _():
                        block = (at * 2 + 1 - low, fsdp)
                        landed(block)
                        for kind in self.across:
                            self.visit(kind, block, False, action)
        if 3 in self.across:
            other = (1 - fsdp // 2) * 2 + fsdp % 2
            for step in range(2 * self.line):
                block = ((ctx + step) % (2 * self.line), other)
                landed(block)
                self.visit(4, block, False, action)
            for step in range(2 * self.line):
                for x in range(2):
                    landed(((ctx + step) % (2 * self.line), x * 2 + 1 - fsdp % 2))

    def go(self, after_first=None):
        self.run(lambda copy: copy.start(), self.arrive, after_first)

    def finish(self):
        self.run(lambda copy: copy.wait_send(), lambda block: None)


def spread_kernel(
    rows_ref, weight_ref, out_ref, all_ref, mine_ref, theirs_ref,
    sends, recvs, w_sends, w_recvs, o_sems, local,
):
    ctx, fsdp = lax.axis_index("ctx"), lax.axis_index("fsdp")
    slabs = lax.axis_size("ctx")
    rows, features = rows_ref.shape
    kinds, depth, share = weight_ref.shape
    width = share // slabs
    others = [((ctx + step) % slabs, fsdp) for step in range(1, slabs)]
    x, core = fsdp // 2, fsdp % 2
    meet(others + [(ctx, (1 - x) * 2 + core), (ctx, x * 2 + 1 - core)])

    def place(slab, part):
        return all_ref.at[pl.ds(slab * rows, rows), pl.ds(part * features, features)]

    def piece(kind, slab):
        return weight_ref.at[kind, :, pl.ds(slab * width, width)]

    def landing(kind, slab):
        return mine_ref.at[pl.ds(slab * depth, depth), pl.ds(kind * width, width)]

    own = [pltpu.make_async_copy(rows_ref, place(ctx, fsdp), local.at[0])] + [
        pltpu.make_async_copy(piece(kind, ctx), landing(kind, ctx), local.at[1 + kind])
        for kind in range(kinds)
    ]

    def weight_copies(owner, source, target):
        return [
            pltpu.make_async_remote_copy(
                src_ref=piece(kind, target),
                dst_ref=landing(kind, source),
                send_sem=w_sends.at[target, kind],
                recv_sem=w_recvs.at[source, kind],
                device_id=(owner, fsdp),
                device_id_type=MESH,
            )
            for kind in range(kinds)
        ]

    line, high, low = slabs // 2, ctx // 2, ctx % 2

    def send_to(target):
        for copy in weight_copies(target, ctx, target):
            copy.start()

    def send_weights(away):
        hold = line - 1
        for goal in range(line if away >= hold else 0):
            below, above = high, line - 1 - high
            up = ((below <= away) if away == hold else (below == away)) & (goal > high)
            down = ((above <= away) if away == hold else (above == away)) & (goal < high)

            @pl.when(up | down)
            def _():
                send_to(goal * 2 + low)

        if away == line - 1:
            for step in range(line):
                send_to((high + step) % line * 2 + 1 - low)

    swap = pltpu.make_async_remote_copy(
        src_ref=out_ref,
        dst_ref=theirs_ref,
        send_sem=o_sems.at[0],
        recv_sem=o_sems.at[1],
        device_id=(ctx, x * 2 + 1 - core),
        device_id_type=MESH,
    )
    relay = Relay(rows_ref, place, sends, recvs, (3, 4))
    for copy in own:
        copy.start()
    swap.start()
    relay.go(send_weights)
    for step in range(1, slabs):
        source = (ctx + step) % slabs
        for copy in weight_copies(source, source, source):
            copy.wait_recv()
    relay.finish()
    for step in range(1, slabs):
        target = (ctx + step) % slabs
        for copy in weight_copies(target, ctx, target):
            copy.wait_send()
    swap.wait()
    for copy in own:
        copy.wait()


def collect_kernel(cols_ref, all_ref, other_ref, sends, recvs, half_recvs, local):
    ctx, fsdp = lax.axis_index("ctx"), lax.axis_index("fsdp")
    slabs, parts = lax.axis_size("ctx"), lax.axis_size("fsdp")
    width = cols_ref.shape[2]
    x, core = fsdp // 2, fsdp % 2
    partner = (ctx, x * 2 + 1 - core)
    meet([((ctx + step) % slabs, fsdp) for step in range(1, slabs)] + [partner])

    def place(slab, part):
        return all_ref.at[:, :, pl.ds(slab * width, width)]

    def half(block, own):
        cols = pl.ds(block[0] * width, width)
        return pltpu.make_async_remote_copy(
            src_ref=cols_ref.at[1 - core] if own else all_ref.at[1 - core, :, cols],
            dst_ref=other_ref.at[:, cols],
            send_sem=sends.at[3, block[0] * parts + fsdp],
            recv_sem=half_recvs.at[block[0]],
            device_id=partner,
            device_id_type=MESH,
        )

    own = pltpu.make_async_copy(cols_ref, place(ctx, fsdp), local.at[0])
    own.start()
    relay = Relay(cols_ref, place, sends, recvs, (4,), half)
    relay.go()
    for step in range(slabs):
        half(((ctx + step) % slabs, fsdp), False).wait_recv()
    relay.finish()
    own.wait()


def deliver_kernel(terms_ref, out_ref, sends, recvs, local):
    ctx, fsdp = lax.axis_index("ctx"), lax.axis_index("fsdp")
    slabs, parts = lax.axis_size("ctx"), lax.axis_size("fsdp")
    fold = slabs // parts
    width = terms_ref.shape[2]
    x, core = fsdp // 2, fsdp % 2
    home = ctx // fold
    stays = (home == fsdp) & (ctx % 2 == core)
    targets = [(ctx // 2 + step) % (slabs // 2) for step in range(slabs // 2)]
    sources = [(half, other) for half in range(fold) for other in range(parts // 2)]

    def to_others(action):
        for high in targets:
            @pl.when(jnp.logical_not(stays & (high == ctx // 2)))
            def _():
                action(high, (high * 2 + core, home))

    def from_others(action):
        for half, other in sources:
            source = (fsdp * fold + half, other * 2 + ctx % 2)

            @pl.when(jnp.logical_not((source[0] == ctx) & (source[1] == fsdp)))
            def _():
                action(half, other, source)

    barrier = pltpu.get_barrier_semaphore()

    def greet(device):
        pl.semaphore_signal(barrier, inc=1, device_id=device, device_id_type=MESH)

    to_others(lambda high, device: greet(device))
    from_others(lambda half, other, device: greet(device))

    @pl.when(stays)
    def _():
        pl.semaphore_wait(barrier, len(targets) + len(sources) - 2)

    @pl.when(jnp.logical_not(stays))
    def _():
        pl.semaphore_wait(barrier, len(targets) + len(sources))

    def slot(half, other):
        return out_ref.at[other, :, pl.ds(half * width, width)]

    def outgoing(high, device):
        return pltpu.make_async_remote_copy(
            src_ref=terms_ref.at[high],
            dst_ref=slot(ctx % fold, x),
            send_sem=sends.at[high],
            recv_sem=recvs.at[x * fold + ctx % fold],
            device_id=device,
            device_id_type=MESH,
        )

    def incoming(half, other, device):
        return pltpu.make_async_remote_copy(
            src_ref=terms_ref.at[0],
            dst_ref=slot(half, other),
            send_sem=sends.at[0],
            recv_sem=recvs.at[other * fold + half],
            device_id=device,
            device_id_type=MESH,
        )

    own = pltpu.make_async_copy(terms_ref.at[ctx // 2], slot(ctx % fold, x), local.at[0])
    to_others(lambda high, device: outgoing(high, device).start())

    @pl.when(stays)
    def _():
        own.start()

    from_others(lambda half, other, device: incoming(half, other, device).wait_recv())
    to_others(lambda high, device: outgoing(high, device).wait_send())

    @pl.when(stays)
    def _():
        own.wait()


VMEM_SPEC = pl.BlockSpec(memory_space=pltpu.VMEM)
ANY_SPEC = pl.BlockSpec(memory_space=pl.ANY)
DMA = pltpu.SemaphoreType.DMA


def params(number):
    return pltpu.CompilerParams(collective_id=number, has_side_effects=True)


def spread(rows, weights, out_weight):
    slabs, parts = lax.axis_size("ctx"), lax.axis_size("fsdp")
    kinds, depth, share = weights.shape
    return pl.pallas_call(
        spread_kernel,
        out_shape=(
            jax.ShapeDtypeStruct((rows.shape[0] * slabs, rows.shape[1] * parts), rows.dtype),
            jax.ShapeDtypeStruct((depth * slabs, kinds * share // slabs), weights.dtype),
            jax.ShapeDtypeStruct(out_weight.shape, out_weight.dtype),
        ),
        in_specs=[VMEM_SPEC, VMEM_SPEC, VMEM_SPEC],
        out_specs=(ANY_SPEC, ANY_SPEC, ANY_SPEC),
        scratch_shapes=[
            DMA((5, slabs * parts)), DMA((slabs * parts,)),
            DMA((slabs, kinds)), DMA((slabs, kinds)), DMA((2,)), DMA((1 + kinds,)),
        ],
        compiler_params=params(0),
    )(rows, weights, out_weight)


def collect(cols):
    slabs, parts = lax.axis_size("ctx"), lax.axis_size("fsdp")
    halves, rows, width = cols.shape
    return pl.pallas_call(
        collect_kernel,
        out_shape=(
            jax.ShapeDtypeStruct((halves, rows, width * slabs), cols.dtype),
            jax.ShapeDtypeStruct((rows, width * slabs), cols.dtype),
        ),
        in_specs=[VMEM_SPEC],
        out_specs=(ANY_SPEC, ANY_SPEC),
        scratch_shapes=[DMA((5, slabs * parts)), DMA((slabs * parts,)), DMA((slabs,)), DMA((1,))],
        compiler_params=params(1),
    )(cols)


def deliver(terms):
    slabs, parts = lax.axis_size("ctx"), lax.axis_size("fsdp")
    fold = slabs // parts
    return pl.pallas_call(
        deliver_kernel,
        out_shape=jax.ShapeDtypeStruct((parts // 2, terms.shape[1], terms.shape[2] * fold), terms.dtype),
        in_specs=[VMEM_SPEC],
        out_specs=ANY_SPEC,
        scratch_shapes=[DMA((slabs // 2,)), DMA((fold * parts // 2,)), DMA((1,))],
        compiler_params=params(2),
    )(terms)


def mix_kernel(
    group_width, rows_ref, weight_ref, taps_ref, base_ref, skip_ref, out_ref, bands, tail, last
):
    groups, window = base_ref.shape
    flen = window // 2
    own = out_ref.shape[2]

    @pl.when(pl.program_id(0) == 0)
    def _():
        tail[...] = jnp.zeros_like(tail)
        last[...] = jnp.zeros_like(last)
        for group in range(groups):
            row = jnp.broadcast_to(base_ref[group : group + 1, :], (flen, window))
            band = pltpu.roll(row, 0, 1, stride=1, stride_axis=0)
            bands[pl.ds(group * flen, flen), :] = band.astype(jnp.bfloat16)

    proj = jnp.dot(rows_ref[...], weight_ref[...], preferred_element_type=jnp.float32)
    proj = proj.astype(jnp.bfloat16).astype(jnp.float32)
    rows = proj.shape[0]
    ahead = tail.shape[0]
    extended = jnp.concatenate([tail[...], proj], axis=0)
    tail[...] = proj[rows - ahead :]
    filtered = short_conv(
        [taps_ref[tap : tap + 1, :] for tap in range(3)], extended[ahead - 2 :]
    )
    product = (filtered[:, own : 2 * own] * filtered[:, 2 * own :]).astype(jnp.bfloat16)
    reach = jnp.concatenate([last[...], product], axis=0)
    last[...] = product[rows - flen :]
    lane_group = lax.broadcasted_iota(jnp.int32, (flen, own), 1) // group_width
    for start in range(0, rows, flen):
        every = jnp.dot(
            bands[...], reach[start : start + window], preferred_element_type=jnp.float32
        )
        conv = every[:flen]
        for group in range(1, groups):
            conv = jnp.where(lane_group == group, every[group * flen : (group + 1) * flen], conv)
        here = product[start : start + flen].astype(jnp.float32)
        gate = filtered[start : start + flen, :own]
        out_ref[0, start : start + flen, :] = (gate * (conv + skip_ref[...] * here)).astype(jnp.bfloat16)


def mix(whole, weights, taps, base, skip, slab_rows, group_width):
    positions, depth = whole.shape
    own = skip.shape[1]
    groups, window = base.shape
    full = lambda array: pl.BlockSpec(array.shape, lambda i: (0, 0))
    return pl.pallas_call(
        functools.partial(mix_kernel, group_width),
        grid=(positions // slab_rows,),
        out_shape=jax.ShapeDtypeStruct((2, positions // 2, own), jnp.bfloat16),
        in_specs=[
            pl.BlockSpec((slab_rows, depth), lambda i: (i, 0)),
            full(weights), full(taps), full(base), full(skip),
        ],
        out_specs=pl.BlockSpec((1, slab_rows, own), lambda i: (i % 2, i // 2, 0)),
        scratch_shapes=[
            pltpu.VMEM((groups * window // 2, window), jnp.bfloat16),
            pltpu.VMEM((8, 3 * own), jnp.float32),
            pltpu.VMEM((window // 2, own), jnp.bfloat16),
        ],
    )(whole, weights, taps, base, skip)


def channel_plan(tokens, norm_gain, in_weight, short_filter, long_filter, skip_gain, out_weight):
    ctx, fsdp = lax.axis_index("ctx"), lax.axis_index("fsdp")
    slabs, parts = lax.axis_size("ctx"), lax.axis_size("fsdp")
    rows, features = tokens.shape
    positions = rows * slabs
    share = in_weight.shape[2]
    own = share // slabs
    values = tokens.astype(jnp.float32)
    mean_square = lax.psum(jnp.sum(values * values, axis=-1, keepdims=True), "fsdp") / (features * parts)
    gain = lax.dynamic_slice_in_dim(norm_gain, fsdp * features, features, 0)
    normed = (values * lax.rsqrt(mean_square + 1e-06) * gain).astype(jnp.bfloat16)

    whole, weights, partner_weight = spread(normed, in_weight.transpose(1, 0, 2), out_weight)
    taps = lax.dynamic_slice_in_dim(short_filter, ctx * own, own, 2).reshape(3, 3 * own)
    flen = long_filter.shape[1]
    group_count = long_filter.shape[0] // slabs
    filters = lax.dynamic_slice_in_dim(long_filter, ctx * group_count, group_count, 0)
    base = jnp.pad(filters[:, ::-1].astype(jnp.float32), ((0, 0), (1, flen - 1)))
    skip = lax.dynamic_slice_in_dim(skip_gain, ctx * own, own, 0)[None]
    gated = mix(whole, weights, taps, base, skip, rows, own // group_count)
    every, partner_cols = collect(gated)
    core_cols = lax.dynamic_index_in_dim(every, fsdp % 2, 0, keepdims=False)
    terms = jnp.dot(core_cols, out_weight, preferred_element_type=jnp.float32)
    terms += jnp.dot(partner_cols, partner_weight, preferred_element_type=jnp.float32)
    terms = terms.astype(jnp.bfloat16).reshape(slabs // 2, rows, out_weight.shape[1])
    arrived = deliver(terms)
    return jnp.sum(arrived.astype(jnp.float32), axis=0).astype(jnp.bfloat16)


def on_device(tokens, *rest):
    slabs, parts = lax.axis_size("ctx"), lax.axis_size("fsdp")
    own = rest[1].shape[2] // slabs
    gathered = tokens.size * slabs * parts * 2
    fits = parts == 4 and slabs % parts == 0 and own % LANE == 0 and gathered <= 2**25
    return (channel_plan if fits else slab_plan)(tokens, *rest)


def solution(mesh):
    in_specs = (
        P("ctx", "fsdp"),
        P(),
        P("ctx", None, "fsdp"),
        P(None, None, "fsdp"),
        P("fsdp", None),
        P("fsdp"),
        P("fsdp", "ctx"),
    )
    out_specs = P("ctx", "fsdp")
    return jax.shard_map(
        on_device, mesh=mesh, in_specs=in_specs, out_specs=out_specs, check_vma=False
    )
```
